128 devices in a mesh: cols: 128 (over x, z, y, core).
Axes of the slice: x: 4, y: 4, z: 4, core: 2. Of those that a mesh axis runs over, the one named last changes fastest.
Arguments:
- suction_initial: float32 [128, 65536], P(None, 'cols'), may hold values from -6 to 6
- warmth_initial: float32 [128, 65536], P(None, 'cols'), may hold values from -5 to 5
- soil_class: int32 [128, 65536], P(None, 'cols'), may hold values from 0 to 7
- top_boundary_warmth: float32 [65536], P('cols'), may hold values from -6 to 6
- neighbour_couplings: int32 [2, 512], replicated, may hold values from 0 to 1
- k_sat: float32 [8], replicated, may hold values from 0.1 to 1
- heat_cond: float32 [8], replicated, may hold values from 0.5 to 2
Outputs:
- suction_iterated: float32 [128, 65536], P(None, 'cols')
- warmth_iterated: float32 [128, 65536], P(None, 'cols')
The draws below stay inside these ranges and needn't reach their ends.
All inputs are finite; a program needn't handle non-finite values.
Results may differ from the reference program's by a relative error of at most 0.000066.
Values sent between devices are 32-bit elements; how exact they have to be, the bound alone decides.
A program may use at most 128 MiB of HBM per device.

```python
import jax
import jax.numpy as jnp
from jax import lax

SOIL_SLABS = 128
UNIT_SPAN = 256
BLK_DEV = 2
PER_STEP = 1
CLASSES = 8
ITERS = 2
PAIR_DEV = 4
COLS = 65536
PAIRS = 512
N_COLS = 128


def chosen_blocks(key):
    number_of_blocks = COLS // UNIT_SPAN
    picks = jax.random.randint(jax.random.fold_in(key, 7), (number_of_blocks,), 0, 8)
    extra = jax.random.randint(jax.random.fold_in(key, 8), (), 0, number_of_blocks)
    positions = jnp.arange(number_of_blocks, dtype=jnp.int32)
    marked = jnp.logical_or(picks == 0, positions == extra)
    return jnp.repeat(marked, UNIT_SPAN)[None, :]


def draw_suction_initial(key, part):
    marked = chosen_blocks(key)
    value_key = jax.random.fold_in(key, 11)
    wet_key = jax.random.fold_in(key, 12)
    spread = jnp.clip(1.5 * jax.random.normal(value_key, (SOIL_SLABS, COLS), jnp.float32), -6.0, 6.0)
    wet = jax.random.uniform(wet_key, (SOIL_SLABS, COLS), jnp.float32, 5.5, 6.0)
    return jnp.where(marked, wet, spread)


def draw_warmth_initial(key, part):
    marked = chosen_blocks(key)
    value_key = jax.random.fold_in(key, 21)
    warm_key = jax.random.fold_in(key, 22)
    spread = jnp.clip(jax.random.normal(value_key, (SOIL_SLABS, COLS), jnp.float32), -5.0, 5.0)
    warm = jax.random.uniform(warm_key, (SOIL_SLABS, COLS), jnp.float32, 2.0, 5.0)
    return jnp.where(marked, warm, spread)


def draw_k_sat(key, part):
    value_key = jax.random.fold_in(key, 31)
    exponent = jax.random.uniform(value_key, (CLASSES,), jnp.float32, -2.302585, 0.0)
    return jnp.exp(exponent)


def set_ends(values, key, least, largest):
    place = [jax.random.randint(jax.random.fold_in(key, axis), (), 0, length) for axis, length in enumerate(values.shape)]
    main_axis = values.shape.index(max(values.shape))
    next_to = place[:main_axis] + [(place[main_axis] + 1) % values.shape[main_axis]] + place[main_axis + 1:]
    return values.at[tuple(place)].set(least).at[tuple(next_to)].set(largest)


def steps_of(rng, dims, pieces, low, high):
    factor_of = 1.0
    for dim, parts in pieces:
        heights = jax.random.uniform(jax.random.fold_in(jax.random.fold_in(rng, 6), dim), (parts,), jnp.float32, low / len(pieces), high / len(pieces))
        factor_of = factor_of * jnp.repeat(jnp.exp(heights), dims[dim] // parts).reshape((-1,) + (1,) * (len(dims) - 1 - dim))
    return factor_of


def centred(key, dims, scale, most, pieces=(), kind=jnp.bfloat16):
    entries = scale * jax.random.normal(key, dims, jnp.float32)
    if pieces:
        entries = entries * steps_of(key, dims, pieces, -0.22, 0.18)
    return jnp.clip(entries, -most, most).astype(kind)


def setup_inputs(seed: int = 0) -> dict:
    seeds = jax.random.split(jax.random.key(seed), 8)
    return {
        "suction_initial": draw_suction_initial(jax.random.fold_in(seeds[7], 71), 0),
        "warmth_initial": draw_warmth_initial(jax.random.fold_in(seeds[7], 71), 0),
        "soil_class": set_ends(jax.random.randint(seeds[2], (SOIL_SLABS, COLS), 0, CLASSES), jax.random.fold_in(seeds[2], 1), 0, CLASSES - 1).astype(jnp.int32),
        "top_boundary_warmth": centred(seeds[3], (COLS,), 1.5, 6.0, ((0, 128),), jnp.float32),
        "neighbour_couplings": set_ends(jax.random.randint(seeds[4], (2, PAIRS), 0, BLK_DEV), jax.random.fold_in(seeds[4], 1), 0, BLK_DEV - 1).astype(jnp.int32),
        "k_sat": draw_k_sat(jax.random.fold_in(seeds[7], 71), 0),
        "heat_cond": jnp.clip(jax.random.uniform(seeds[6], (CLASSES,), jnp.float32, 0.5, 2.0), 0.5, 2.0),
    }


TIME_STEP = 0.5
MELTING_SPECIFIC = 2.0
LATERAL = 0.5
SLOPE = 0.5
CARRY = 2.0


def moisture_of(suction_iterated):
    return 0.05 + 0.4 * jax.nn.sigmoid(suction_iterated)


def passage_coefficient(suction_iterated, warmth_iterated, permeability_profile):
    saturation = jax.nn.sigmoid(suction_iterated)
    melted_portion = jax.nn.sigmoid(2.0 * warmth_iterated)
    return permeability_profile * (melted_portion * saturation * saturation + 0.02)


def below_pad(face):
    return jnp.concatenate([face, jnp.zeros_like(face[:1])], axis=0)


def above_pad(face):
    return jnp.concatenate([jnp.zeros_like(face[:1]), face], axis=0)


def thomas(left_coef, main_coef, right_coef, source):
    zero_row = jnp.zeros_like(main_coef[0])

    def forward(carry, row):
        prev_ratio, prev_value = carry
        left_row, main_row, right_row, source_row = row
        pivot = main_row - left_row * prev_ratio
        ratio_new = right_row / pivot
        value_new = (source_row - left_row * prev_value) / pivot
        return (ratio_new, value_new), (ratio_new, value_new)

    _, (ratios, values) = lax.scan(forward, (zero_row, zero_row), (left_coef, main_coef, right_coef, source))

    def backward(later, row):
        ratio_row, value_row = row
        result = value_row - ratio_row * later
        return result, result

    _, solved = lax.scan(backward, zero_row, (ratios, values), reverse=True)
    return solved


def water_update(suction_iterated, suction_initial, passing_coefficient, side_seepage_inflow):
    saturation = jax.nn.sigmoid(suction_iterated)
    storage_now = 0.05 + 0.4 * saturation
    storage_old = moisture_of(suction_initial)
    boundary_coefficient = 0.5 * (passing_coefficient[:-1] + passing_coefficient[1:])
    descending_motion = -boundary_coefficient * (suction_iterated[1:] - suction_iterated[:-1] - 1.0)
    residual = (storage_now - storage_old) / TIME_STEP + below_pad(descending_motion) - above_pad(descending_motion) - side_seepage_inflow
    capacity = 0.4 * saturation * (1.0 - saturation) + 0.01
    face_above = above_pad(boundary_coefficient)
    face_below = below_pad(boundary_coefficient)
    main_coef = capacity / TIME_STEP + face_above + face_below
    difference_amount = thomas(-face_above, main_coef, -face_below, -residual)
    return suction_iterated + difference_amount


def internal_warmth_step(warmth_iterated, suction_after, warmth_initial, suction_initial, warmth_passing_profile, top_boundary_warmth, side_warmth_inflow):
    dampness_after = moisture_of(suction_after)
    moisture_old = moisture_of(suction_initial)
    melted_portion = jax.nn.sigmoid(2.0 * warmth_iterated)
    liquid_old = jax.nn.sigmoid(2.0 * warmth_initial)
    internal_warmth_new = (1.0 + 2.0 * dampness_after) * warmth_iterated + MELTING_SPECIFIC * dampness_after * melted_portion
    energy_old = (1.0 + 2.0 * moisture_old) * warmth_initial + MELTING_SPECIFIC * moisture_old * liquid_old
    warmth_related = warmth_passing_profile * (1.5 - 0.5 * melted_portion)
    boundary_coefficient = 0.5 * (warmth_related[:-1] + warmth_related[1:])
    descending_motion = -boundary_coefficient * (warmth_iterated[1:] - warmth_iterated[:-1])
    top_boundary_inflow = 2.0 * warmth_related[0] * (top_boundary_warmth - warmth_iterated[0])
    inflow = jnp.concatenate([top_boundary_inflow[None], descending_motion], axis=0)
    residual = (internal_warmth_new - energy_old) / TIME_STEP + below_pad(descending_motion) - inflow - side_warmth_inflow
    apparent = 1.0 + 2.0 * dampness_after + MELTING_SPECIFIC * dampness_after * 2.0 * melted_portion * (1.0 - melted_portion)
    surface_row = jnp.concatenate([2.0 * warmth_related[:1], jnp.zeros_like(warmth_related[1:])], axis=0)
    face_above = above_pad(boundary_coefficient)
    face_below = below_pad(boundary_coefficient)
    main_coef = apparent / TIME_STEP + face_above + face_below + surface_row
    difference_amount = thomas(-face_above, main_coef, -face_below, -residual)
    return warmth_iterated + difference_amount


def pair_flux(upper_prof, lower_prof):
    mean_cond = 0.5 * LATERAL * (upper_prof[2] + lower_prof[2])
    flow = mean_cond * (upper_prof[0] - lower_prof[0] + SLOPE)
    carried = CARRY * (jnp.maximum(flow, 0.0) * upper_prof[1] + jnp.minimum(flow, 0.0) * lower_prof[1])
    return flow, carried


def side_inflow_terms(suction_iterated, warmth_iterated, passing_coefficient, neighbour_couplings):
    number_of_tiles = BLK_DEV * N_COLS
    profile_variables = jnp.stack([suction_iterated, warmth_iterated, passing_coefficient]).reshape(3, SOIL_SLABS, number_of_tiles, UNIT_SPAN)
    water = jnp.zeros((SOIL_SLABS, number_of_tiles, UNIT_SPAN), jnp.float32)
    heat = jnp.zeros((SOIL_SLABS, number_of_tiles, UNIT_SPAN), jnp.float32)
    processor_units = jnp.arange(N_COLS, dtype=jnp.int32)
    for index in range(PAIR_DEV):
        distance = index // PER_STEP + 1
        valid = (processor_units + distance < N_COLS).astype(jnp.float32)[None, :, None]
        upper_blocks = processor_units * BLK_DEV + neighbour_couplings[0, processor_units * PAIR_DEV + index]
        lower_dev = jnp.minimum(processor_units + distance, N_COLS - 1)
        lower_blocks = lower_dev * BLK_DEV + neighbour_couplings[1, processor_units * PAIR_DEV + index]
        flow, carried = pair_flux(profile_variables[:, :, upper_blocks], profile_variables[:, :, lower_blocks])
        flow = flow * valid
        carried = carried * valid
        water = water.at[:, upper_blocks].add(-flow).at[:, lower_blocks].add(flow)
        heat = heat.at[:, upper_blocks].add(-carried).at[:, lower_blocks].add(carried)
    return water.reshape(SOIL_SLABS, number_of_tiles * UNIT_SPAN), heat.reshape(SOIL_SLABS, number_of_tiles * UNIT_SPAN)


def reference(suction_initial, warmth_initial, soil_class, top_boundary_warmth, neighbour_couplings, k_sat, heat_cond):
    permeability_profile = k_sat[soil_class]
    warmth_passing_profile = heat_cond[soil_class]
    suction_iterated = suction_initial
    warmth_iterated = warmth_initial
    for iteration in range(ITERS):
        passing_coefficient = passage_coefficient(suction_iterated, warmth_iterated, permeability_profile)
        side_seepage_inflow, side_warmth_inflow = side_inflow_terms(suction_iterated, warmth_iterated, passing_coefficient, neighbour_couplings)
        suction_after = water_update(suction_iterated, suction_initial, passing_coefficient, side_seepage_inflow)
        warmth_iterated = internal_warmth_step(warmth_iterated, suction_after, warmth_initial, suction_initial, warmth_passing_profile, top_boundary_warmth, side_warmth_inflow)
        suction_iterated = suction_after
    return suction_iterated, warmth_iterated
```

```python
import functools

import jax
import jax.numpy as jnp
from jax import lax
from jax.experimental import pallas as pl
from jax.experimental.pallas import tpu as pltpu
from jax.sharding import PartitionSpec as P

MESH = pl.DeviceIdType.MESH

SPAN = 256
LANES = 128
HALVES = SPAN // LANES
BLOCKS = 2
ROWS = 128
CHUNK = 16
PAIR_DEV = 4

W, P1, M1, P1X, M1X, P2, M2, X2 = range(8)
SLOTS = 8
MESSAGES = 10


def sig(v):
    return 1.0 / (1.0 + jnp.exp(-v))


def message(step, half, field):
    return half * 3 + field if step == 0 else 6 + half * 2 + field


def lookup(table, classes):
    result = jnp.full(classes.shape, table[0], jnp.float32)
    for entry in range(1, table.shape[0]):
        result = jnp.where(classes == entry, table[entry], result)
    return result


def down(value):
    return pltpu.roll(value, 1, 1)


def up(value):
    return pltpu.roll(value, 7, 1)


def strided(row):
    return pl.ds(row, 8, stride=CHUNK)


def forward_row(row, coef, main, above, below, source, carry):
    c_ref, a_ref, d_ref = coef
    c_prev, a_prev, d_prev = carry
    inverse = 1.0 / (main + above * c_prev)
    c_new = -below * inverse
    a_new = above * a_prev * inverse
    d_new = (source + above * d_prev) * inverse
    c_ref[row] = c_new
    a_ref[row] = a_new
    d_ref[row] = d_new
    return c_new, a_new, d_new


def finish(coef, last, write):
    c_ref, a_ref, d_ref = coef
    c_last, a_last, d_last = last
    zero = jnp.zeros_like(c_last)

    def gather(step, carry):
        d_sum, a_sum, g_sum = carry
        row = CHUNK - 2 - step
        c_row = c_ref[row]
        return d_ref[row] - c_row * d_sum, a_ref[row] - c_row * a_sum, -c_row * g_sum

    d_sum, a_sum, g_sum = lax.fori_loop(0, CHUNK - 1, gather, (zero, zero, zero - 1.0), unroll=True)
    inverse = 1.0 / (1.0 - c_last * up(a_sum))
    alpha = a_last * inverse
    gamma = -c_last * up(g_sum) * inverse
    delta = (d_last - c_last * up(d_sum)) * inverse
    for shift in (1, 2, 4):
        back = functools.partial(pltpu.roll, shift=shift, axis=1)
        ahead = functools.partial(pltpu.roll, shift=8 - shift, axis=1)
        inverse = 1.0 / (1.0 - alpha * back(gamma) - gamma * ahead(alpha))
        delta = (delta - alpha * back(delta) - gamma * ahead(delta)) * inverse
        if shift < 4:
            alpha, gamma = -alpha * back(alpha) * inverse, -gamma * ahead(gamma) * inverse
    before = down(delta)
    write(CHUNK - 1, delta)

    def back_row(step, later):
        row = CHUNK - 2 - step
        value = (d_ref[row] - a_ref[row] * before) - c_ref[row] * later
        write(row, value)
        return value

    lax.fori_loop(0, CHUNK - 1, back_row, delta, unroll=True)


def kernel(
    devices,
    head_hbm,
    warmth_hbm,
    class_hbm,
    top_ref,
    couplings,
    k_table,
    lam_table,
    head_out,
    warmth_out,
    own,
    rx,
    result,
    classes,
    lam,
    sat,
    melt,
    cond,
    energy_old,
    lat_water,
    lat_heat,
    c_ref,
    a_ref,
    d_ref,
    load_sem,
    store_sem,
    send_sem,
    recv_sem,
):
    me = lax.axis_index("cols")
    core = lax.rem(me, 2)
    other = me + 1 - 2 * core
    ahead = lax.rem(me + 2, devices)
    behind = lax.rem(me + devices - 2, devices)
    coef = (c_ref, a_ref, d_ref)

    def columns(half, block):
        return pl.ds(block * SPAN + half * LANES, LANES)

    def load(half, field, block):
        source = (head_hbm, warmth_hbm, class_hbm)[field]
        target = classes.at[half, block] if field == 2 else own.at[message(0, half, field), block]
        return pltpu.make_async_copy(
            source.at[:, columns(half, block)], target, load_sem.at[half, field, block]
        )

    def store(half, field, block):
        target = (head_out, warmth_out)[field]
        return pltpu.make_async_copy(
            result.at[half, field, block],
            target.at[:, columns(half, block)],
            store_sem.at[half, field, block],
        )

    def copy(slot, index):
        if slot in (W, P1, M1):
            source = own.at[index]
        elif slot in (P1X, P2):
            source = rx.at[P1, index]
        elif slot in (M1X, M2):
            source = rx.at[M1, index]
        else:
            source = rx.at[M2 - core * (M2 - P2), index]
        target = {P1: ahead, P2: ahead, M1: behind, M2: behind}.get(slot, other)
        return pltpu.make_async_remote_copy(
            src_ref=source,
            dst_ref=rx.at[slot, index],
            send_sem=send_sem.at[slot, index],
            recv_sem=recv_sem.at[slot, index],
            device_id=(target,),
            device_id_type=MESH,
        )

    def lookups(half):
        def body(tile, carry):
            rows = pl.ds(pl.multiple_of(tile * 8, 8), 8)
            for block in range(BLOCKS):
                kinds = classes[half, block, rows, :]
                own[message(0, half, 2), block, rows, :] = lookup(k_table, kinds)
                lam[half, block, rows, :] = lookup(lam_table, kinds)
            return carry

        lax.fori_loop(0, ROWS // 8, body, 0)

    def prepare(step, half):
        def body(tile, carry):
            rows = pl.ds(pl.multiple_of(tile * 8, 8), 8)
            for block in range(BLOCKS):
                head = own[message(step, half, 0), block, rows, :]
                warmth = own[message(step, half, 1), block, rows, :]
                filled = sig(head)
                liquid = sig(2.0 * warmth)
                sat[step, half, block, rows, :] = filled
                melt[half, block, rows, :] = liquid
                cond[half, block, rows, :] = own[message(0, half, 2), block, rows, :] * (
                    liquid * filled * filled + 0.02
                )
                if step == 0:
                    moist = 0.05 + 0.4 * filled
                    energy_old[half, block, rows, :] = (
                        1.0 + 2.0 * moist
                    ) * warmth + 2.0 * moist * liquid
            return carry

        lax.fori_loop(0, ROWS // 8, body, 0)

    def pair_of(slot):
        upper = {M1: 1, M1X: 1, M2: 1, P1: 0, P1X: 0, P2: 0, W: 1 - core, X2: core}[slot]
        distance = {
            M1: 2, P1: 2, M2: 4, P2: 4, W: 1, X2: 3, M1X: 3 - 2 * core, P1X: 1 + 2 * core
        }[slot]
        first = me - (1 - upper) * distance
        valid = jnp.logical_and(first >= 0, first + distance < devices).astype(jnp.int32)
        pair = lax.rem(first + devices, devices) * PAIR_DEV + distance - 1
        return upper, pair, valid

    def lateral(step, half, slots, first):
        settings = []
        for slot in slots:
            upper, pair, valid = pair_of(slot)
            mine = couplings[1 - upper, pair]
            theirs = couplings[upper, pair]
            slope = jnp.full((8, LANES), upper.astype(jnp.float32) - 0.5 if not isinstance(upper, int) else upper - 0.5)
            mine = jnp.full((8, LANES), mine, jnp.int32) == 1
            theirs = jnp.full((8, LANES), theirs, jnp.int32) == 1
            live = jnp.full((8, LANES), valid, jnp.int32) == 1
            settings.append((slot, slope, mine, theirs, live))

        def body(tile, carry):
            rows = pl.ds(pl.multiple_of(tile * 8, 8), 8)
            heads = [own[message(step, half, 0), block, rows, :] for block in range(BLOCKS)]
            warmths = [own[message(step, half, 1), block, rows, :] for block in range(BLOCKS)]
            conds = [cond[half, block, rows, :] for block in range(BLOCKS)]
            zero = jnp.zeros((8, LANES), jnp.float32)
            if first:
                water = [zero, zero]
                heat = [zero, zero]
            else:
                water = [lat_water[half, block, rows, :] for block in range(BLOCKS)]
                heat = [lat_heat[half, block, rows, :] for block in range(BLOCKS)]
            for slot, slope, mine, theirs, live in settings:

                def far(field, at):
                    index = message(at, half, field)
                    return jnp.where(theirs, rx[slot, index, 1, rows, :], rx[slot, index, 0, rows, :])

                far_head, far_warmth, far_k = far(0, step), far(1, step), far(2, 0)
                filled = sig(far_head)
                far_cond = far_k * (sig(2.0 * far_warmth) * filled * filled + 0.02)
                near_head = jnp.where(mine, heads[1], heads[0])
                near_warmth = jnp.where(mine, warmths[1], warmths[0])
                near_cond = jnp.where(mine, conds[1], conds[0])
                flow = 0.25 * (near_cond + far_cond) * (near_head - far_head + slope)
                flow = jnp.where(live, flow, 0.0)
                carried = 2.0 * (
                    jnp.maximum(flow, 0.0) * near_warmth + jnp.minimum(flow, 0.0) * far_warmth
                )
                water[0] = water[0] - jnp.where(mine, 0.0, flow)
                water[1] = water[1] - jnp.where(mine, flow, 0.0)
                heat[0] = heat[0] - jnp.where(mine, 0.0, carried)
                heat[1] = heat[1] - jnp.where(mine, carried, 0.0)
            for block in range(BLOCKS):
                lat_water[half, block, rows, :] = water[block]
                lat_heat[half, block, rows, :] = heat[block]
            return carry

        lax.fori_loop(0, ROWS // 8, body, 0)

    sublane = lax.broadcasted_iota(jnp.int32, (BLOCKS, 8, LANES), 1)
    is_top = sublane == 0

    def new_head(step, half, row):
        if step == 0:
            return own[message(1, half, 0), :, strided(row), :]
        return result[half, 0, :, strided(row), :]

    def water(step, half):
        index = message(step, half, 0)

        def cond_row(row):
            return cond[half, :, strided(row), :]

        def head_row(row):
            return own[index, :, strided(row), :]

        def one(row, k_above, q_above, k_below, q_below, carry):
            filled = sat[step, half, :, strided(row), :]
            source = lat_water[half, :, strided(row), :] + q_above - q_below
            if step > 0:
                source = source - 0.8 * (filled - sat[0, half, :, strided(row), :])
            main = 0.8 * filled * (1.0 - filled) + 0.02 + k_above + k_below
            return forward_row(row, coef, main, k_above, k_below, source, carry)

        zero = jnp.zeros((BLOCKS, 8, LANES), jnp.float32)
        cond_first, head_first = cond_row(0), head_row(0)
        k_first = jnp.where(is_top, 0.0, 0.5 * (down(cond_row(CHUNK - 1)) + cond_first))
        q_first = -k_first * (head_first - down(head_row(CHUNK - 1)) - 1.0)

        def body(row, carry):
            cond_here, head_here, k_above, q_above, *chain = carry
            cond_next, head_next = cond_row(row + 1), head_row(row + 1)
            k_below = 0.5 * (cond_here + cond_next)
            q_below = -k_below * (head_next - head_here - 1.0)
            chain = one(row, k_above, q_above, k_below, q_below, chain)
            return (cond_next, head_next, k_below, q_below, *chain)

        start = (cond_first, head_first, k_first, q_first, zero, zero - 1.0, zero)
        _, _, k_above, q_above, *chain = lax.fori_loop(0, CHUNK - 1, body, start, unroll=True)
        last = one(CHUNK - 1, k_above, q_above, up(k_first), up(q_first), chain)

        def write(row, change):
            value = head_row(row) + change
            if step == 0:
                own[message(1, half, 0), :, strided(row), :] = value
            else:
                result[half, 0, :, strided(row), :] = value

        finish(coef, last, write)

    def energy(step, half):
        index = message(step, half, 1)

        def warmth_row(row):
            return own[index, :, strided(row), :]

        def passing_row(row):
            return lam[half, :, strided(row), :] * (1.5 - 0.5 * melt[half, :, strided(row), :])

        def one(row, here, extra, k_above, q_above, k_below, q_below, carry):
            moist = 0.05 + 0.4 * sig(new_head(step, half, row))
            liquid = melt[half, :, strided(row), :]
            slack = 1.0 + 2.0 * moist
            stored = slack * here + 2.0 * moist * liquid
            source = (
                lat_heat[half, :, strided(row), :]
                + q_above
                - q_below
                - 2.0 * (stored - energy_old[half, :, strided(row), :])
            )
            main = 2.0 * (slack + 4.0 * moist * liquid * (1.0 - liquid)) + k_above + k_below
            if extra is not None:
                main = main + extra
            return forward_row(row, coef, main, k_above, k_below, source, carry)

        zero = jnp.zeros((BLOCKS, 8, LANES), jnp.float32)
        passing_first, warmth_first = passing_row(0), warmth_row(0)
        top = jnp.stack(
            [
                jnp.broadcast_to(top_ref[pl.ds(block * HALVES + half, 1), :], (8, LANES))
                for block in range(BLOCKS)
            ]
        )
        k_first = jnp.where(is_top, 0.0, 0.5 * (down(passing_row(CHUNK - 1)) + passing_first))
        q_first = -k_first * (warmth_first - down(warmth_row(CHUNK - 1)))
        surface = jnp.where(is_top, 2.0 * passing_first, 0.0)
        q_surface = q_first + surface * (top - warmth_first)

        def body(row, carry):
            passing_here, warmth_here, extra, k_above, q_above, *chain = carry
            passing_next, warmth_next = passing_row(row + 1), warmth_row(row + 1)
            k_below = 0.5 * (passing_here + passing_next)
            q_below = -k_below * (warmth_next - warmth_here)
            chain = one(row, warmth_here, extra, k_above, q_above, k_below, q_below, chain)
            return (passing_next, warmth_next, zero, k_below, q_below, *chain)

        start = (passing_first, warmth_first, surface, k_first, q_surface, zero, zero - 1.0, zero)
        _, here, _, k_above, q_above, *chain = lax.fori_loop(0, CHUNK - 1, body, start, unroll=True)
        last = one(CHUNK - 1, here, None, k_above, q_above, up(k_first), up(q_first), chain)

        def write(row, change):
            value = warmth_row(row) + change
            if step == 0:
                own[message(1, half, 1), :, strided(row), :] = value
            else:
                result[half, 1, :, strided(row), :] = value

        finish(coef, last, write)

    def send_own(index):
        for slot in (P1, M1, W):
            copy(slot, index).start()

    def relay(index):
        copy(P1, index).wait_recv()
        copy(P2, index).start()
        copy(P1X, index).start()
        copy(M1, index).wait_recv()
        copy(M2, index).start()
        copy(M1X, index).start()

    def forward(index):
        copy(P2, index).wait_recv()
        copy(M2, index).wait_recv()
        copy(X2, index).start()

    def arrived(slot, indices):
        for index in indices:
            copy(slot, index).wait_recv()

    def first_sends(half):
        for field in range(2):
            for block in range(BLOCKS):
                load(half, field, block).wait()
            send_own(message(0, half, field))
        for block in range(BLOCKS):
            load(half, 2, block).wait()
        lookups(half)
        send_own(message(0, half, 2))

    def indices_of(step, half):
        return [message(step, half, field) for field in range(3 if step == 0 else 2)]

    def near(step, half):
        indices = indices_of(step, half)
        for index in indices:
            relay(index)

    def rest(step, half):
        indices = indices_of(step, half)
        arrived(W, indices)
        lateral(step, half, (W, P1, M1), True)
        for index in indices:
            forward(index)
        arrived(P1X, indices)
        arrived(M1X, indices)
        lateral(step, half, (P1X, M1X, P2, M2), False)
        arrived(X2, indices)
        lateral(step, half, (X2,), False)
        water(step, half)
        energy(step, half)

    for half in range(HALVES):
        for field in range(3):
            for block in range(BLOCKS):
                load(half, field, block).start()

    barrier = pltpu.get_barrier_semaphore()
    for device in (other, ahead, behind):
        pl.semaphore_signal(barrier, inc=1, device_id=(device,), device_id_type=MESH)
    pl.semaphore_wait(barrier, 3)

    first_sends(0)
    prepare(0, 0)
    near(0, 0)
    first_sends(1)
    prepare(0, 1)
    rest(0, 0)
    near(0, 1)
    for index in indices_of(1, 0):
        send_own(index)
    prepare(1, 0)
    rest(0, 1)
    near(1, 0)
    for index in indices_of(1, 1):
        send_own(index)
    prepare(1, 1)
    rest(1, 0)
    for field in range(2):
        for block in range(BLOCKS):
            store(0, field, block).start()
    near(1, 1)
    rest(1, 1)
    for field in range(2):
        for block in range(BLOCKS):
            store(1, field, block).start()
    for slot in range(SLOTS):
        for index in range(MESSAGES):
            copy(slot, index).wait_send()
    for half in range(HALVES):
        for field in range(2):
            for block in range(BLOCKS):
                store(half, field, block).wait()


def solution(mesh):
    devices = mesh.shape["cols"]

    def on_device(head, warmth, kinds, top, couplings, k_sat, heat_cond):
        plane = (BLOCKS, ROWS, LANES)
        anywhere = pl.BlockSpec(memory_space=pl.ANY)
        vector = pl.BlockSpec(memory_space=pltpu.VMEM)
        scalar = pl.BlockSpec(memory_space=pltpu.SMEM)
        f32 = jnp.float32
        out = jax.ShapeDtypeStruct(head.shape, f32)
        return pl.pallas_call(
            functools.partial(kernel, devices),
            out_shape=(out, out),
            in_specs=[anywhere, anywhere, anywhere, vector, scalar, scalar, scalar],
            out_specs=(anywhere, anywhere),
            scratch_shapes=[
                pltpu.VMEM((MESSAGES,) + plane, f32),
                pltpu.VMEM((SLOTS, MESSAGES) + plane, f32),
                pltpu.VMEM((HALVES, 2) + plane, f32),
                pltpu.VMEM((HALVES,) + plane, jnp.int32),
                pltpu.VMEM((HALVES,) + plane, f32),
                pltpu.VMEM((2, HALVES) + plane, f32),
                pltpu.VMEM((HALVES,) + plane, f32),
                pltpu.VMEM((HALVES,) + plane, f32),
                pltpu.VMEM((HALVES,) + plane, f32),
                pltpu.VMEM((HALVES,) + plane, f32),
                pltpu.VMEM((HALVES,) + plane, f32),
                pltpu.VMEM((CHUNK, BLOCKS, 8, LANES), f32),
                pltpu.VMEM((CHUNK, BLOCKS, 8, LANES), f32),
                pltpu.VMEM((CHUNK, BLOCKS, 8, LANES), f32),
                pltpu.SemaphoreType.DMA((HALVES, 3, BLOCKS)),
                pltpu.SemaphoreType.DMA((HALVES, 2, BLOCKS)),
                pltpu.SemaphoreType.DMA((SLOTS, MESSAGES)),
                pltpu.SemaphoreType.DMA((SLOTS, MESSAGES)),
            ],
            compiler_params=pltpu.CompilerParams(
                collective_id=0, has_side_effects=True, vmem_limit_bytes=32 * 1024 * 1024
            ),
        )(head, warmth, kinds, top.reshape(BLOCKS * HALVES, LANES), couplings, k_sat, heat_cond)

    placed = (P(None, "cols"), P(None, "cols"), P(None, "cols"), P("cols"), P(), P(), P())
    return jax.shard_map(
        on_device,
        mesh=mesh,
        in_specs=placed,
        out_specs=(P(None, "cols"), P(None, "cols")),
        check_vma=False,
    )
```

```python
import functools

import jax
import jax.numpy as jnp
from jax import lax
from jax.experimental import pallas as pl
from jax.experimental.pallas import tpu as pltpu
from jax.sharding import PartitionSpec as P

MESH = pl.DeviceIdType.MESH

SPAN = 256
LANES = 128
HALVES = SPAN // LANES
BLOCKS = 2
ROWS = 128
CHUNK = 16
PAIR_DEV = 4

W, P1, M1, P1X, M1X, P2, M2, X2 = range(8)
SLOTS = 8
P1B, M1B, Y2 = 8, 9, 10
COPIES = 11
MESSAGES = 10


def sig(v):
    return 1.0 / (1.0 + jnp.exp(-v))


def message(step, half, field):
    return half * 3 + field if step == 0 else 6 + half * 2 + field


def lookup(table, classes):
    result = jnp.full(classes.shape, table[0], jnp.float32)
    for entry in range(1, table.shape[0]):
        result = jnp.where(classes == entry, table[entry], result)
    return result


def down(value):
    return pltpu.roll(value, 1, 1)


def up(value):
    return pltpu.roll(value, 7, 1)


def strided(row):
    return pl.ds(row, 8, stride=CHUNK)


def forward_row(row, coef, main, above, below, source, carry):
    c_ref, a_ref, d_ref = coef
    c_prev, a_prev, d_prev = carry
    inverse = 1.0 / (main + above * c_prev)
    c_new = -below * inverse
    a_new = above * a_prev * inverse
    d_new = (source + above * d_prev) * inverse
    c_ref[row] = c_new
    a_ref[row] = a_new
    d_ref[row] = d_new
    return c_new, a_new, d_new


def finish(coef, last, write):
    c_ref, a_ref, d_ref = coef
    c_last, a_last, d_last = last
    zero = jnp.zeros_like(c_last)

    def gather(step, carry):
        d_sum, a_sum, g_sum = carry
        row = CHUNK - 2 - step
        c_row = c_ref[row]
        return d_ref[row] - c_row * d_sum, a_ref[row] - c_row * a_sum, -c_row * g_sum

    d_sum, a_sum, g_sum = lax.fori_loop(0, CHUNK - 1, gather, (zero, zero, zero - 1.0), unroll=True)
    inverse = 1.0 / (1.0 - c_last * up(a_sum))
    alpha = a_last * inverse
    gamma = -c_last * up(g_sum) * inverse
    delta = (d_last - c_last * up(d_sum)) * inverse
    for shift in (1, 2, 4):
        back = functools.partial(pltpu.roll, shift=shift, axis=1)
        ahead = functools.partial(pltpu.roll, shift=8 - shift, axis=1)
        inverse = 1.0 / (1.0 - alpha * back(gamma) - gamma * ahead(alpha))
        delta = (delta - alpha * back(delta) - gamma * ahead(delta)) * inverse
        if shift < 4:
            alpha, gamma = -alpha * back(alpha) * inverse, -gamma * ahead(gamma) * inverse
    before = down(delta)
    write(CHUNK - 1, delta)

    def back_row(step, later):
        row = CHUNK - 2 - step
        value = (d_ref[row] - a_ref[row] * before) - c_ref[row] * later
        write(row, value)
        return value

    lax.fori_loop(0, CHUNK - 1, back_row, delta, unroll=True)


def kernel(
    devices,
    head_hbm,
    warmth_hbm,
    class_hbm,
    top_ref,
    couplings,
    k_table,
    lam_table,
    head_out,
    warmth_out,
    own,
    rx,
    result,
    classes,
    lam,
    sat,
    melt,
    cond,
    energy_old,
    lat_water,
    lat_heat,
    c_ref,
    a_ref,
    d_ref,
    load_sem,
    store_sem,
    send_sem,
    recv_sem,
):
    me = lax.axis_index("cols")
    core = lax.rem(me, 2)
    other = me + 1 - 2 * core
    ahead = lax.rem(me + 2, devices)
    behind = lax.rem(me + devices - 2, devices)
    chips = devices // 2
    chip = me // 2
    coef = (c_ref, a_ref, d_ref)

    def columns(half, block):
        return pl.ds(block * SPAN + half * LANES, LANES)

    def load(half, field, block):
        source = (head_hbm, warmth_hbm, class_hbm)[field]
        target = classes.at[half, block] if field == 2 else own.at[0, message(0, half, field), block]
        return pltpu.make_async_copy(
            source.at[:, columns(half, block)], target, load_sem.at[half, field, block]
        )

    def store(half, field, block):
        target = (head_out, warmth_out)[field]
        return pltpu.make_async_copy(
            result.at[half, field, block],
            target.at[:, columns(half, block)],
            store_sem.at[half, field, block],
        )

    def copy(kind, index):
        if kind == W:
            source, target, device = own.at[0, index], rx.at[W, index], other
        elif kind in (P1, P1B):
            block = int(kind == P1B)
            source, target, device = own.at[1 - core, index, block], rx.at[P1, index, block], ahead
        elif kind in (M1, M1B):
            block = int(kind == M1B)
            source, target, device = own.at[core, index, block], rx.at[M1, index, block], behind
        elif kind == P1X:
            source, target, device = rx.at[P1, index], rx.at[P1X, index], other
        elif kind == M1X:
            source, target, device = rx.at[M1, index], rx.at[M1X, index], other
        elif kind == P2:
            source, target, device = rx.at[P1, index, 0], rx.at[P2, index, 0], ahead
        elif kind == M2:
            source, target, device = rx.at[M1, index, 0], rx.at[M2, index, 0], behind
        elif kind == Y2:
            source = rx.at[M1 - core * (M1 - P1), index, 1]
            target = rx.at[M2 - core * (M2 - P2), index, 1]
            device = behind + core * (ahead - behind)
        else:
            source, target, device = rx.at[M2 - core * (M2 - P2), index], rx.at[X2, index], other
        return pltpu.make_async_remote_copy(
            src_ref=source,
            dst_ref=target,
            send_sem=send_sem.at[kind, index],
            recv_sem=recv_sem.at[kind, index],
            device_id=(device,),
            device_id_type=MESH,
        )

    far_two = core * (chip >= 2) + (1 - core) * (chip <= chips - 3)
    far_two_other = (1 - core) * (chip >= 2) + core * (chip <= chips - 3)
    below, above = chip >= 1, chip <= chips - 2
    middle = jnp.logical_and(below, above)
    sends = {
        W: None, P1: above, P1B: above, M1: below, M1B: below, P1X: below, M1X: above,
        P2: middle, M2: middle, Y2: middle, X2: far_two == 1,
    }
    receives = {
        W: None, P1: below, P1B: below, M1: above, M1B: above, P1X: below, M1X: above,
        P2: chip >= 2, M2: chip <= chips - 3, Y2: far_two == 1, X2: far_two_other == 1,
    }

    def guarded(condition, action):
        if condition is None:
            action()
        else:
            pl.when(condition)(action)

    def start(kind, *indices):
        def action():
            for index in indices:
                copy(kind, index).start()

        guarded(sends[kind], action)

    def arrive(kind, *indices):
        def action():
            for index in indices:
                copy(kind, index).wait_recv()

        guarded(receives[kind], action)

    def order_of(device, side):
        pair = (device - side * lax.min(device, 4)) * PAIR_DEV + 3
        return couplings[side, pair]

    def order(index):
        swap = jnp.full((8, LANES), order_of(me, core), jnp.int32) == 1

        def body(tile, carry):
            rows = pl.ds(pl.multiple_of(tile * 8, 8), 8)
            zeroth = own[0, index, 0, rows, :]
            oneth = own[0, index, 1, rows, :]
            own[1, index, 0, rows, :] = jnp.where(swap, oneth, zeroth)
            own[1, index, 1, rows, :] = jnp.where(swap, zeroth, oneth)
            return carry

        lax.fori_loop(0, ROWS // 8, body, 0, unroll=4)

    def clear():
        missing = (
            (chip < 1, (P1, P1X)), (chip < 2, (P2,)), (chip > chips - 2, (M1, M1X)), (chip > chips - 3, (M2,)),
            (far_two_other == 0, (X2,)),
        )
        for condition, slots in missing:

            def action(slots=slots):
                def body(index, carry):
                    for slot in slots:
                        rx[slot, index] = jnp.zeros((BLOCKS, ROWS, LANES), jnp.float32)
                    return carry

                lax.fori_loop(0, MESSAGES, body, 0)

            pl.when(condition)(action)

    def lookups(half):
        def body(tile, carry):
            rows = pl.ds(pl.multiple_of(tile * 8, 8), 8)
            for block in range(BLOCKS):
                kinds = classes[half, block, rows, :]
                own[0, message(0, half, 2), block, rows, :] = lookup(k_table, kinds)
                lam[half, block, rows, :] = lookup(lam_table, kinds)
            return carry

        lax.fori_loop(0, ROWS // 8, body, 0)

    def prepare(step, half):
        def body(tile, carry):
            rows = pl.ds(pl.multiple_of(tile * 8, 8), 8)
            for block in range(BLOCKS):
                head = own[0, message(step, half, 0), block, rows, :]
                warmth = own[0, message(step, half, 1), block, rows, :]
                filled = sig(head)
                liquid = sig(2.0 * warmth)
                sat[step, half, block, rows, :] = filled
                melt[half, block, rows, :] = liquid
                cond[half, block, rows, :] = own[0, message(0, half, 2), block, rows, :] * (
                    liquid * filled * filled + 0.02
                )
                if step == 0:
                    moist = 0.05 + 0.4 * filled
                    energy_old[half, block, rows, :] = (
                        1.0 + 2.0 * moist
                    ) * warmth + 2.0 * moist * liquid
            return carry

        lax.fori_loop(0, ROWS // 8, body, 0)

    def pair_of(slot):
        upper = {M1: 1, M1X: 1, M2: 1, P1: 0, P1X: 0, P2: 0, W: 1 - core, X2: core}[slot]
        distance = {
            M1: 2, P1: 2, M2: 4, P2: 4, W: 1, X2: 3, M1X: 3 - 2 * core, P1X: 1 + 2 * core
        }[slot]
        sender = me + (2 * upper - 1) * distance
        first = me - (1 - upper) * distance
        valid = jnp.logical_and(first >= 0, first + distance < devices).astype(jnp.int32)
        pair = lax.rem(first + devices, devices) * PAIR_DEV + distance - 1
        ordered = {W: 0, P1: 1 - core, M1: core, P1X: core, M1X: 1 - core, P2: 1 - core, M2: core, X2: 0}[slot]
        sender_core = lax.rem(sender + devices, 2)
        sender = lax.min(lax.max(sender, 0), devices - 1)
        swap = ordered * order_of(sender, sender_core)
        return upper, pair, valid, swap

    def lateral(step, half, slots, first):
        settings = []
        for slot in slots:
            upper, pair, valid, swap = pair_of(slot)
            mine = couplings[1 - upper, pair]
            theirs = couplings[upper, pair] + swap
            slope = jnp.full((8, LANES), upper.astype(jnp.float32) - 0.5 if not isinstance(upper, int) else upper - 0.5)
            mine = jnp.full((8, LANES), mine, jnp.int32) == 1
            theirs = jnp.full((8, LANES), theirs, jnp.int32) == 1
            live = jnp.full((8, LANES), valid, jnp.int32) == 1
            settings.append((slot, slope, mine, theirs, live))

        def body(tile, carry):
            rows = pl.ds(pl.multiple_of(tile * 8, 8), 8)
            heads = [own[0, message(step, half, 0), block, rows, :] for block in range(BLOCKS)]
            warmths = [own[0, message(step, half, 1), block, rows, :] for block in range(BLOCKS)]
            conds = [cond[half, block, rows, :] for block in range(BLOCKS)]
            zero = jnp.zeros((8, LANES), jnp.float32)
            if first:
                water = [zero, zero]
                heat = [zero, zero]
            else:
                water = [lat_water[half, block, rows, :] for block in range(BLOCKS)]
                heat = [lat_heat[half, block, rows, :] for block in range(BLOCKS)]
            for slot, slope, mine, theirs, live in settings:

                def far(field, at):
                    index = message(at, half, field)
                    return jnp.where(theirs, rx[slot, index, 1, rows, :], rx[slot, index, 0, rows, :])

                far_head, far_warmth, far_k = far(0, step), far(1, step), far(2, 0)
                filled = sig(far_head)
                far_cond = far_k * (sig(2.0 * far_warmth) * filled * filled + 0.02)
                near_head = jnp.where(mine, heads[1], heads[0])
                near_warmth = jnp.where(mine, warmths[1], warmths[0])
                near_cond = jnp.where(mine, conds[1], conds[0])
                flow = 0.25 * (near_cond + far_cond) * (near_head - far_head + slope)
                flow = jnp.where(live, flow, 0.0)
                carried = 2.0 * (
                    jnp.maximum(flow, 0.0) * near_warmth + jnp.minimum(flow, 0.0) * far_warmth
                )
                water[0] = water[0] - jnp.where(mine, 0.0, flow)
                water[1] = water[1] - jnp.where(mine, flow, 0.0)
                heat[0] = heat[0] - jnp.where(mine, 0.0, carried)
                heat[1] = heat[1] - jnp.where(mine, carried, 0.0)
            for block in range(BLOCKS):
                lat_water[half, block, rows, :] = water[block]
                lat_heat[half, block, rows, :] = heat[block]
            return carry

        lax.fori_loop(0, ROWS // 8, body, 0)

    sublane = lax.broadcasted_iota(jnp.int32, (BLOCKS, 8, LANES), 1)
    is_top = sublane == 0

    def new_head(step, half, row):
        if step == 0:
            return own[0, message(1, half, 0), :, strided(row), :]
        return result[half, 0, :, strided(row), :]

    def water(step, half):
        index = message(step, half, 0)

        def cond_row(row):
            return cond[half, :, strided(row), :]

        def head_row(row):
            return own[0, index, :, strided(row), :]

        def one(row, k_above, q_above, k_below, q_below, carry):
            filled = sat[step, half, :, strided(row), :]
            source = lat_water[half, :, strided(row), :] + q_above - q_below
            if step > 0:
                source = source - 0.8 * (filled - sat[0, half, :, strided(row), :])
            main = 0.8 * filled * (1.0 - filled) + 0.02 + k_above + k_below
            return forward_row(row, coef, main, k_above, k_below, source, carry)

        zero = jnp.zeros((BLOCKS, 8, LANES), jnp.float32)
        cond_first, head_first = cond_row(0), head_row(0)
        k_first = jnp.where(is_top, 0.0, 0.5 * (down(cond_row(CHUNK - 1)) + cond_first))
        q_first = -k_first * (head_first - down(head_row(CHUNK - 1)) - 1.0)

        def body(row, carry):
            cond_here, head_here, k_above, q_above, *chain = carry
            cond_next, head_next = cond_row(row + 1), head_row(row + 1)
            k_below = 0.5 * (cond_here + cond_next)
            q_below = -k_below * (head_next - head_here - 1.0)
            chain = one(row, k_above, q_above, k_below, q_below, chain)
            return (cond_next, head_next, k_below, q_below, *chain)

        start = (cond_first, head_first, k_first, q_first, zero, zero - 1.0, zero)
        _, _, k_above, q_above, *chain = lax.fori_loop(0, CHUNK - 1, body, start, unroll=True)
        last = one(CHUNK - 1, k_above, q_above, up(k_first), up(q_first), chain)

        def write(row, change):
            value = head_row(row) + change
            if step == 0:
                own[0, message(1, half, 0), :, strided(row), :] = value
            else:
                result[half, 0, :, strided(row), :] = value

        finish(coef, last, write)

    def energy(step, half):
        index = message(step, half, 1)

        def warmth_row(row):
            return own[0, index, :, strided(row), :]

        def passing_row(row):
            return lam[half, :, strided(row), :] * (1.5 - 0.5 * melt[half, :, strided(row), :])

        def one(row, here, extra, k_above, q_above, k_below, q_below, carry):
            moist = 0.05 + 0.4 * sig(new_head(step, half, row))
            liquid = melt[half, :, strided(row), :]
            slack = 1.0 + 2.0 * moist
            stored = slack * here + 2.0 * moist * liquid
            source = (
                lat_heat[half, :, strided(row), :]
                + q_above
                - q_below
                - 2.0 * (stored - energy_old[half, :, strided(row), :])
            )
            main = 2.0 * (slack + 4.0 * moist * liquid * (1.0 - liquid)) + k_above + k_below
            if extra is not None:
                main = main + extra
            return forward_row(row, coef, main, k_above, k_below, source, carry)

        zero = jnp.zeros((BLOCKS, 8, LANES), jnp.float32)
        passing_first, warmth_first = passing_row(0), warmth_row(0)
        top = jnp.stack(
            [
                jnp.broadcast_to(top_ref[pl.ds(block * HALVES + half, 1), :], (8, LANES))
                for block in range(BLOCKS)
            ]
        )
        k_first = jnp.where(is_top, 0.0, 0.5 * (down(passing_row(CHUNK - 1)) + passing_first))
        q_first = -k_first * (warmth_first - down(warmth_row(CHUNK - 1)))
        surface = jnp.where(is_top, 2.0 * passing_first, 0.0)
        q_surface = q_first + surface * (top - warmth_first)

        def body(row, carry):
            passing_here, warmth_here, extra, k_above, q_above, *chain = carry
            passing_next, warmth_next = passing_row(row + 1), warmth_row(row + 1)
            k_below = 0.5 * (passing_here + passing_next)
            q_below = -k_below * (warmth_next - warmth_here)
            chain = one(row, warmth_here, extra, k_above, q_above, k_below, q_below, chain)
            return (passing_next, warmth_next, zero, k_below, q_below, *chain)

        start = (passing_first, warmth_first, surface, k_first, q_surface, zero, zero - 1.0, zero)
        _, here, _, k_above, q_above, *chain = lax.fori_loop(0, CHUNK - 1, body, start, unroll=True)
        last = one(CHUNK - 1, here, None, k_above, q_above, up(k_first), up(q_first), chain)

        def write(row, change):
            value = warmth_row(row) + change
            if step == 0:
                own[0, message(1, half, 1), :, strided(row), :] = value
            else:
                result[half, 1, :, strided(row), :] = value

        finish(coef, last, write)

    def send_own(index):
        start(W, index)
        order(index)
        start(P1, index)
        start(M1, index)
        start(P1B, index)
        start(M1B, index)

    def first_sends(half):
        for field in range(2):
            for block in range(BLOCKS):
                load(half, field, block).wait()
            send_own(message(0, half, field))
        for block in range(BLOCKS):
            load(half, 2, block).wait()
        lookups(half)
        send_own(message(0, half, 2))

    def indices_of(step, half):
        return [message(step, half, field) for field in range(3 if step == 0 else 2)]

    def relay(step, half):
        for index in indices_of(step, half):
            arrive(P1, index)
            start(P2, index)
            arrive(M1, index)
            start(M2, index)
            arrive(P1B, index)
            arrive(M1B, index)
            start(Y2, index)
            start(P1X, index)
            start(M1X, index)

    def early(step, half):
        arrive(W, *indices_of(step, half))
        lateral(step, half, (W, P1, M1), True)

    def late(step, half):
        indices = indices_of(step, half)
        arrive(P1X, *indices)
        arrive(M1X, *indices)
        lateral(step, half, (P1X, M1X), False)
        for index in indices:
            arrive(P2, index)
            arrive(M2, index)
            arrive(Y2, index)
            start(X2, index)
        lateral(step, half, (P2, M2), False)
        arrive(X2, *indices)
        lateral(step, half, (X2,), False)
        water(step, half)
        energy(step, half)

    def second_sends(half):
        for index in indices_of(1, half):
            send_own(index)

    for half in range(HALVES):
        for field in range(3):
            for block in range(BLOCKS):
                load(half, field, block).start()

    barrier = pltpu.get_barrier_semaphore()
    pl.semaphore_signal(barrier, inc=1, device_id=(other,), device_id_type=MESH)

    @pl.when(above)
    def _():
        pl.semaphore_signal(barrier, inc=1, device_id=(ahead,), device_id_type=MESH)

    @pl.when(below)
    def _():
        pl.semaphore_signal(barrier, inc=1, device_id=(behind,), device_id_type=MESH)

    pl.semaphore_wait(barrier, 1 + above.astype(jnp.int32) + below.astype(jnp.int32))

    first_sends(0)
    prepare(0, 0)
    clear()
    relay(0, 0)
    first_sends(1)
    prepare(0, 1)
    early(0, 0)
    late(0, 0)
    second_sends(0)
    relay(0, 1)
    prepare(1, 0)
    early(0, 1)
    relay(1, 0)
    late(0, 1)
    second_sends(1)
    prepare(1, 1)
    early(1, 0)
    relay(1, 1)
    late(1, 0)
    for field in range(2):
        for block in range(BLOCKS):
            store(0, field, block).start()
    early(1, 1)
    late(1, 1)
    for field in range(2):
        for block in range(BLOCKS):
            store(1, field, block).start()
    for kind in range(COPIES):

        def action(kind=kind):
            for index in range(MESSAGES):
                copy(kind, index).wait_send()

        guarded(sends[kind], action)
    for half in range(HALVES):
        for field in range(2):
            for block in range(BLOCKS):
                store(half, field, block).wait()


def solution(mesh):
    devices = mesh.shape["cols"]

    def on_device(head, warmth, kinds, top, couplings, k_sat, heat_cond):
        plane = (BLOCKS, ROWS, LANES)
        anywhere = pl.BlockSpec(memory_space=pl.ANY)
        hbm = pl.BlockSpec(memory_space=pltpu.HBM)
        vector = pl.BlockSpec(memory_space=pltpu.VMEM)
        scalar = pl.BlockSpec(memory_space=pltpu.SMEM)
        f32 = jnp.float32
        out = jax.ShapeDtypeStruct(head.shape, f32)
        return pl.pallas_call(
            functools.partial(kernel, devices),
            out_shape=(out, out),
            in_specs=[hbm, hbm, hbm, vector, scalar, scalar, scalar],
            out_specs=(anywhere, anywhere),
            scratch_shapes=[
                pltpu.VMEM((2, MESSAGES) + plane, f32),
                pltpu.VMEM((SLOTS, MESSAGES) + plane, f32),
                pltpu.VMEM((HALVES, 2) + plane, f32),
                pltpu.VMEM((HALVES,) + plane, jnp.int32),
                pltpu.VMEM((HALVES,) + plane, f32),
                pltpu.VMEM((2, HALVES) + plane, f32),
                pltpu.VMEM((HALVES,) + plane, f32),
                pltpu.VMEM((HALVES,) + plane, f32),
                pltpu.VMEM((HALVES,) + plane, f32),
                pltpu.VMEM((HALVES,) + plane, f32),
                pltpu.VMEM((HALVES,) + plane, f32),
                pltpu.VMEM((CHUNK, BLOCKS, 8, LANES), f32),
                pltpu.VMEM((CHUNK, BLOCKS, 8, LANES), f32),
                pltpu.VMEM((CHUNK, BLOCKS, 8, LANES), f32),
                pltpu.SemaphoreType.DMA((HALVES, 3, BLOCKS)),
                pltpu.SemaphoreType.DMA((HALVES, 2, BLOCKS)),
                pltpu.SemaphoreType.DMA((COPIES, MESSAGES)),
                pltpu.SemaphoreType.DMA((COPIES, MESSAGES)),
            ],
            compiler_params=pltpu.CompilerParams(
                collective_id=0, has_side_effects=True, vmem_limit_bytes=67043328
            ),
        )(head, warmth, kinds, top.reshape(BLOCKS * HALVES, LANES), couplings, k_sat, heat_cond)

    placed = (P(None, "cols"), P(None, "cols"), P(None, "cols"), P("cols"), P(), P(), P())
    return jax.shard_map(
        on_device,
        mesh=mesh,
        in_specs=placed,
        out_specs=(P(None, "cols"), P(None, "cols")),
        check_vma=False,
    )
```

```python
import functools

import jax
import jax.numpy as jnp
from jax import lax
from jax.experimental import pallas as pl
from jax.experimental.pallas import tpu as pltpu
from jax.sharding import PartitionSpec as P

MESH = pl.DeviceIdType.MESH

SPAN = 256
LANES = 128
HALVES = SPAN // LANES
BLOCKS = 2
ROWS = 128
CHUNK = 16
PAIR_DEV = 4

W, P1, M1, P1X, M1X, P2, M2, X2 = range(8)
SLOTS = 8
P1B, M1B = 8, 9
COPIES = 10
NATURAL, UPWARD, DOWNWARD = range(3)
MESSAGES = 10


def sig(v):
    return 1.0 / (1.0 + jnp.exp(-v))


def message(step, half, field):
    return half * 3 + field if step == 0 else 6 + half * 2 + field


def lookup(table, classes):
    result = jnp.full(classes.shape, table[0], jnp.float32)
    for entry in range(1, table.shape[0]):
        result = jnp.where(classes == entry, table[entry], result)
    return result


def down(value):
    return pltpu.roll(value, 1, 1)


def up(value):
    return pltpu.roll(value, 7, 1)


def strided(row):
    return pl.ds(row, 8, stride=CHUNK)


def forward_row(row, coef, main, above, below, source, carry):
    c_ref, a_ref, d_ref = coef
    c_prev, a_prev, d_prev = carry
    inverse = 1.0 / (main + above * c_prev)
    c_new = -below * inverse
    a_new = above * a_prev * inverse
    d_new = (source + above * d_prev) * inverse
    c_ref[row] = c_new
    a_ref[row] = a_new
    d_ref[row] = d_new
    return c_new, a_new, d_new


def finish(coef, last, write):
    c_ref, a_ref, d_ref = coef
    c_last, a_last, d_last = last
    zero = jnp.zeros_like(c_last)

    def gather(step, carry):
        d_sum, a_sum, g_sum = carry
        row = CHUNK - 2 - step
        c_row = c_ref[row]
        return d_ref[row] - c_row * d_sum, a_ref[row] - c_row * a_sum, -c_row * g_sum

    d_sum, a_sum, g_sum = lax.fori_loop(0, CHUNK - 1, gather, (zero, zero, zero - 1.0), unroll=True)
    inverse = 1.0 / (1.0 - c_last * up(a_sum))
    alpha = a_last * inverse
    gamma = -c_last * up(g_sum) * inverse
    delta = (d_last - c_last * up(d_sum)) * inverse
    for shift in (1, 2, 4):
        back = functools.partial(pltpu.roll, shift=shift, axis=1)
        ahead = functools.partial(pltpu.roll, shift=8 - shift, axis=1)
        inverse = 1.0 / (1.0 - alpha * back(gamma) - gamma * ahead(alpha))
        delta = (delta - alpha * back(delta) - gamma * ahead(delta)) * inverse
        if shift < 4:
            alpha, gamma = -alpha * back(alpha) * inverse, -gamma * ahead(gamma) * inverse
    before = down(delta)
    write(CHUNK - 1, delta)

    def back_row(step, later):
        row = CHUNK - 2 - step
        value = (d_ref[row] - a_ref[row] * before) - c_ref[row] * later
        write(row, value)
        return value

    lax.fori_loop(0, CHUNK - 1, back_row, delta, unroll=True)


def kernel(
    devices,
    head_hbm,
    warmth_hbm,
    class_hbm,
    top_hbm,
    couplings_hbm,
    k_hbm,
    lam_hbm,
    head_out,
    warmth_out,
    own,
    rx,
    passed,
    result,
    classes,
    lam,
    sat,
    melt,
    cond,
    energy_old,
    lat_water,
    lat_heat,
    c_ref,
    a_ref,
    d_ref,
    top_ref,
    couplings,
    k_table,
    lam_table,
    table_sem,
    load_sem,
    store_sem,
    send_sem,
    recv_sem,
):
    me = lax.axis_index("cols")
    core = lax.rem(me, 2)
    other = me + 1 - 2 * core
    ahead = lax.rem(me + 2, devices)
    behind = lax.rem(me + devices - 2, devices)
    across = lax.rem(me + devices - 1 + 2 * core, devices)
    chips = devices // 2
    chip = me // 2
    coef = (c_ref, a_ref, d_ref)

    def columns(half, block):
        return pl.ds(block * SPAN + half * LANES, LANES)

    def load(half, field, block):
        source = (head_hbm, warmth_hbm, class_hbm)[field]
        target = classes.at[half, block] if field == 2 else own.at[NATURAL, message(0, half, field), block]
        return pltpu.make_async_copy(
            source.at[:, columns(half, block)], target, load_sem.at[half, field, block]
        )

    def store(half, field, block):
        target = (head_out, warmth_out)[field]
        return pltpu.make_async_copy(
            result.at[half, field, block],
            target.at[:, columns(half, block)],
            store_sem.at[half, field, block],
        )

    def copy(kind, index):
        if kind == W:
            source, target, device = own.at[NATURAL, index], rx.at[W, index], other
        elif kind in (P1, P1B):
            block = int(kind == P1B)
            source, target, device = own.at[UPWARD, index, block], rx.at[P1, index, block], ahead
        elif kind in (M1, M1B):
            block = int(kind == M1B)
            source, target, device = own.at[DOWNWARD, index, block], rx.at[M1, index, block], behind
        elif kind == P1X:
            source, target, device = rx.at[P1, index], rx.at[P1X, index], other
        elif kind == M1X:
            source, target, device = rx.at[M1, index], rx.at[M1X, index], other
        elif kind == P2:
            source, target, device = rx.at[P1, index, 0], rx.at[P2, index, 0], ahead
        elif kind == M2:
            source, target, device = rx.at[M1, index, 0], rx.at[M2, index, 0], behind
        else:
            source, target, device = passed.at[index], rx.at[X2, index, 0], across
        return pltpu.make_async_remote_copy(
            src_ref=source,
            dst_ref=target,
            send_sem=send_sem.at[kind, index],
            recv_sem=recv_sem.at[kind, index],
            device_id=(device,),
            device_id_type=MESH,
        )

    far_across = core * (chip <= chips - 3) + (1 - core) * (chip >= 2)
    near_across = core * (chip <= chips - 2) + (1 - core) * (chip >= 1)
    below, above = chip >= 1, chip <= chips - 2
    middle = jnp.logical_and(below, above)
    sends = {
        W: None, P1: above, P1B: above, M1: below, M1B: below, P1X: below, M1X: above,
        P2: middle, M2: middle, X2: middle,
    }
    receives = {
        W: None, P1: below, P1B: below, M1: above, M1B: above, P1X: below, M1X: above,
        P2: chip >= 2, M2: chip <= chips - 3, X2: far_across == 1,
    }

    def guarded(condition, action):
        if condition is None:
            action()
        else:
            pl.when(condition)(action)

    def start(kind, *indices):
        def action():
            for index in indices:
                copy(kind, index).start()

        guarded(sends[kind], action)

    def arrive(kind, *indices):
        def action():
            for index in indices:
                copy(kind, index).wait_recv()

        guarded(receives[kind], action)

    def order_of(device, side):
        first = device if side == 0 else lax.max(device - 4, 0)
        return couplings[side, first * PAIR_DEV + 3]

    def mask(value):
        return jnp.full((8, LANES), value, jnp.int32) == 1

    def order(index):
        swaps = [(UPWARD, mask(order_of(me, 0))), (DOWNWARD, mask(order_of(me, 1)))]

        def body(tile, carry):
            rows = pl.ds(pl.multiple_of(tile * 8, 8), 8)
            zeroth = own[NATURAL, index, 0, rows, :]
            oneth = own[NATURAL, index, 1, rows, :]
            for version, swap in swaps:
                own[version, index, 0, rows, :] = jnp.where(swap, oneth, zeroth)
                own[version, index, 1, rows, :] = jnp.where(swap, zeroth, oneth)
            return carry

        lax.fori_loop(0, ROWS // 8, body, 0, unroll=4)

    def passing(index):
        sender = lax.min(lax.max(me + 2 - 4 * core, 0), devices - 1)
        first = lax.max(sender - 3 * (1 - core), 0)
        swap = core * order_of(sender, 0) + (1 - core) * order_of(sender, 1)
        chosen = couplings[1 - core, first * PAIR_DEV + 2] + swap
        chosen = mask(chosen)
        slot = M1 - core * (M1 - P1)

        def body(tile, carry):
            rows = pl.ds(pl.multiple_of(tile * 8, 8), 8)
            passed[index, rows, :] = jnp.where(chosen, rx[slot, index, 1, rows, :], rx[slot, index, 0, rows, :])
            return carry

        lax.fori_loop(0, ROWS // 8, body, 0, unroll=4)

    def clear():
        missing = (
            (chip < 1, (P1, P1X)), (chip < 2, (P2,)), (chip > chips - 2, (M1, M1X)), (chip > chips - 3, (M2,)),
            (far_across == 0, (X2,)),
        )
        for condition, slots in missing:

            def action(slots=slots):
                def body(index, carry):
                    for slot in slots:
                        rx[slot, index] = jnp.zeros((BLOCKS, ROWS, LANES), jnp.float32)
                    return carry

                lax.fori_loop(0, MESSAGES, body, 0)

            pl.when(condition)(action)

    def lookups(half):
        def body(tile, carry):
            rows = pl.ds(pl.multiple_of(tile * 8, 8), 8)
            for block in range(BLOCKS):
                kinds = classes[half, block, rows, :]
                own[NATURAL, message(0, half, 2), block, rows, :] = lookup(k_table, kinds)
                lam[half, block, rows, :] = lookup(lam_table, kinds)
            return carry

        lax.fori_loop(0, ROWS // 8, body, 0)

    def prepare(step, half):
        def body(tile, carry):
            rows = pl.ds(pl.multiple_of(tile * 8, 8), 8)
            for block in range(BLOCKS):
                head = own[NATURAL, message(step, half, 0), block, rows, :]
                warmth = own[NATURAL, message(step, half, 1), block, rows, :]
                filled = sig(head)
                liquid = sig(2.0 * warmth)
                sat[step, half, block, rows, :] = filled
                melt[half, block, rows, :] = liquid
                cond[half, block, rows, :] = own[NATURAL, message(0, half, 2), block, rows, :] * (
                    liquid * filled * filled + 0.02
                )
                if step == 0:
                    moist = 0.05 + 0.4 * filled
                    energy_old[half, block, rows, :] = (
                        1.0 + 2.0 * moist
                    ) * warmth + 2.0 * moist * liquid
            return carry

        lax.fori_loop(0, ROWS // 8, body, 0)

    def pair_of(slot):
        upper = {M1: 1, M1X: 1, M2: 1, P1: 0, P1X: 0, P2: 0, W: 1 - core, X2: core}[slot]
        distance = {
            M1: 2, P1: 2, M2: 4, P2: 4, W: 1, X2: 3, M1X: 3 - 2 * core, P1X: 1 + 2 * core
        }[slot]
        sender = me + (2 * upper - 1) * distance
        first = me - (1 - upper) * distance
        valid = jnp.logical_and(first >= 0, first + distance < devices).astype(jnp.int32)
        pair = lax.rem(first + devices, devices) * PAIR_DEV + distance - 1
        sender = lax.min(lax.max(sender, 0), devices - 1)
        swap = order_of(sender, upper) if isinstance(upper, int) else 0
        return upper, pair, valid, swap

    def lateral(step, half, slots, first):
        settings = []
        for slot in slots:
            upper, pair, valid, swap = pair_of(slot)
            mine = couplings[1 - upper, pair]
            theirs = couplings[upper, pair] + swap
            slope = jnp.full((8, LANES), upper.astype(jnp.float32) - 0.5 if not isinstance(upper, int) else upper - 0.5)
            settings.append((slot, slope, mask(mine), mask(theirs), mask(valid)))

        def body(tile, carry):
            rows = pl.ds(pl.multiple_of(tile * 8, 8), 8)
            heads = [own[NATURAL, message(step, half, 0), block, rows, :] for block in range(BLOCKS)]
            warmths = [own[NATURAL, message(step, half, 1), block, rows, :] for block in range(BLOCKS)]
            conds = [cond[half, block, rows, :] for block in range(BLOCKS)]
            zero = jnp.zeros((8, LANES), jnp.float32)
            if first:
                water = [zero, zero]
                heat = [zero, zero]
            else:
                water = [lat_water[half, block, rows, :] for block in range(BLOCKS)]
                heat = [lat_heat[half, block, rows, :] for block in range(BLOCKS)]
            for slot, slope, mine, theirs, live in settings:

                def far(field, at):
                    index = message(at, half, field)
                    if slot in (P2, M2, X2):
                        return rx[slot, index, 0, rows, :]
                    return jnp.where(theirs, rx[slot, index, 1, rows, :], rx[slot, index, 0, rows, :])

                far_head, far_warmth, far_k = far(0, step), far(1, step), far(2, 0)
                filled = sig(far_head)
                far_cond = far_k * (sig(2.0 * far_warmth) * filled * filled + 0.02)
                near_head = jnp.where(mine, heads[1], heads[0])
                near_warmth = jnp.where(mine, warmths[1], warmths[0])
                near_cond = jnp.where(mine, conds[1], conds[0])
                flow = 0.25 * (near_cond + far_cond) * (near_head - far_head + slope)
                flow = jnp.where(live, flow, 0.0)
                carried = 2.0 * (
                    jnp.maximum(flow, 0.0) * near_warmth + jnp.minimum(flow, 0.0) * far_warmth
                )
                water[0] = water[0] - jnp.where(mine, 0.0, flow)
                water[1] = water[1] - jnp.where(mine, flow, 0.0)
                heat[0] = heat[0] - jnp.where(mine, 0.0, carried)
                heat[1] = heat[1] - jnp.where(mine, carried, 0.0)
            for block in range(BLOCKS):
                lat_water[half, block, rows, :] = water[block]
                lat_heat[half, block, rows, :] = heat[block]
            return carry

        lax.fori_loop(0, ROWS // 8, body, 0)

    sublane = lax.broadcasted_iota(jnp.int32, (BLOCKS, 8, LANES), 1)
    is_top = sublane == 0

    def new_head(step, half, row):
        if step == 0:
            return own[NATURAL, message(1, half, 0), :, strided(row), :]
        return result[half, 0, :, strided(row), :]

    def water(step, half):
        index = message(step, half, 0)

        def cond_row(row):
            return cond[half, :, strided(row), :]

        def head_row(row):
            return own[NATURAL, index, :, strided(row), :]

        def one(row, k_above, q_above, k_below, q_below, carry):
            filled = sat[step, half, :, strided(row), :]
            source = lat_water[half, :, strided(row), :] + q_above - q_below
            if step > 0:
                source = source - 0.8 * (filled - sat[0, half, :, strided(row), :])
            main = 0.8 * filled * (1.0 - filled) + 0.02 + k_above + k_below
            return forward_row(row, coef, main, k_above, k_below, source, carry)

        zero = jnp.zeros((BLOCKS, 8, LANES), jnp.float32)
        cond_first, head_first = cond_row(0), head_row(0)
        k_first = jnp.where(is_top, 0.0, 0.5 * (down(cond_row(CHUNK - 1)) + cond_first))
        q_first = -k_first * (head_first - down(head_row(CHUNK - 1)) - 1.0)

        def body(row, carry):
            cond_here, head_here, k_above, q_above, *chain = carry
            cond_next, head_next = cond_row(row + 1), head_row(row + 1)
            k_below = 0.5 * (cond_here + cond_next)
            q_below = -k_below * (head_next - head_here - 1.0)
            chain = one(row, k_above, q_above, k_below, q_below, chain)
            return (cond_next, head_next, k_below, q_below, *chain)

        start = (cond_first, head_first, k_first, q_first, zero, zero - 1.0, zero)
        _, _, k_above, q_above, *chain = lax.fori_loop(0, CHUNK - 1, body, start, unroll=True)
        last = one(CHUNK - 1, k_above, q_above, up(k_first), up(q_first), chain)

        def write(row, change):
            value = head_row(row) + change
            if step == 0:
                own[NATURAL, message(1, half, 0), :, strided(row), :] = value
            else:
                result[half, 0, :, strided(row), :] = value

        finish(coef, last, write)

    def energy(step, half):
        index = message(step, half, 1)

        def warmth_row(row):
            return own[NATURAL, index, :, strided(row), :]

        def passing_row(row):
            return lam[half, :, strided(row), :] * (1.5 - 0.5 * melt[half, :, strided(row), :])

        def one(row, here, extra, k_above, q_above, k_below, q_below, carry):
            moist = 0.05 + 0.4 * sig(new_head(step, half, row))
            liquid = melt[half, :, strided(row), :]
            slack = 1.0 + 2.0 * moist
            stored = slack * here + 2.0 * moist * liquid
            source = (
                lat_heat[half, :, strided(row), :]
                + q_above
                - q_below
                - 2.0 * (stored - energy_old[half, :, strided(row), :])
            )
            main = 2.0 * (slack + 4.0 * moist * liquid * (1.0 - liquid)) + k_above + k_below
            if extra is not None:
                main = main + extra
            return forward_row(row, coef, main, k_above, k_below, source, carry)

        zero = jnp.zeros((BLOCKS, 8, LANES), jnp.float32)
        passing_first, warmth_first = passing_row(0), warmth_row(0)
        top = jnp.stack(
            [
                jnp.broadcast_to(top_ref[pl.ds(block * HALVES + half, 1), :], (8, LANES))
                for block in range(BLOCKS)
            ]
        )
        k_first = jnp.where(is_top, 0.0, 0.5 * (down(passing_row(CHUNK - 1)) + passing_first))
        q_first = -k_first * (warmth_first - down(warmth_row(CHUNK - 1)))
        surface = jnp.where(is_top, 2.0 * passing_first, 0.0)
        q_surface = q_first + surface * (top - warmth_first)

        def body(row, carry):
            passing_here, warmth_here, extra, k_above, q_above, *chain = carry
            passing_next, warmth_next = passing_row(row + 1), warmth_row(row + 1)
            k_below = 0.5 * (passing_here + passing_next)
            q_below = -k_below * (warmth_next - warmth_here)
            chain = one(row, warmth_here, extra, k_above, q_above, k_below, q_below, chain)
            return (passing_next, warmth_next, zero, k_below, q_below, *chain)

        start = (passing_first, warmth_first, surface, k_first, q_surface, zero, zero - 1.0, zero)
        _, here, _, k_above, q_above, *chain = lax.fori_loop(0, CHUNK - 1, body, start, unroll=True)
        last = one(CHUNK - 1, here, None, k_above, q_above, up(k_first), up(q_first), chain)

        def write(row, change):
            value = warmth_row(row) + change
            if step == 0:
                own[NATURAL, message(1, half, 1), :, strided(row), :] = value
            else:
                result[half, 1, :, strided(row), :] = value

        finish(coef, last, write)

    def send_own(index):
        start(W, index)
        order(index)
        start(P1, index)
        start(M1, index)
        start(P1B, index)
        start(M1B, index)

    def first_sends(half):
        for field in range(2):
            for block in range(BLOCKS):
                load(half, field, block).wait()
            send_own(message(0, half, field))
        for block in range(BLOCKS):
            load(half, 2, block).wait()
        lookups(half)
        send_own(message(0, half, 2))

    def indices_of(step, half):
        return [message(step, half, field) for field in range(3 if step == 0 else 2)]

    def relay(step, half, fields=(0, 1, 2)):
        for index in [message(step, half, field) for field in fields if step == 0 or field < 2]:
            arrive(P1, index)
            start(P2, index)
            arrive(M1, index)
            start(M2, index)
            arrive(P1B, index)
            arrive(M1B, index)
            passing(index)
            start(P1X, index)
            start(M1X, index)
            start(X2, index)

    def early(step, half):
        arrive(W, *indices_of(step, half))
        lateral(step, half, (W, P1, M1), True)

    def late(step, half):
        indices = indices_of(step, half)
        arrive(P1X, *indices)
        arrive(M1X, *indices)
        lateral(step, half, (P1X, M1X), False)
        arrive(P2, *indices)
        arrive(M2, *indices)
        arrive(X2, *indices)
        lateral(step, half, (P2, M2, X2), False)

    def solve(step, half, send=False):
        water(step, half)
        if send:
            send_own(message(1, half, 0))
        energy(step, half)
        if send:
            send_own(message(1, half, 1))

    barrier = pltpu.get_barrier_semaphore()
    pl.semaphore_signal(barrier, inc=1, device_id=(other,), device_id_type=MESH)

    @pl.when(above)
    def _():
        pl.semaphore_signal(barrier, inc=1, device_id=(ahead,), device_id_type=MESH)

    @pl.when(below)
    def _():
        pl.semaphore_signal(barrier, inc=1, device_id=(behind,), device_id_type=MESH)

    @pl.when(near_across == 1)
    def _():
        pl.semaphore_signal(barrier, inc=1, device_id=(across,), device_id_type=MESH)

    for half in range(HALVES):
        for field in range(3):
            for block in range(BLOCKS):
                load(half, field, block).start()
    tables = [
        pltpu.make_async_copy(source, target, table_sem.at[place])
        for place, (source, target) in enumerate(
            ((couplings_hbm, couplings), (k_hbm, k_table), (lam_hbm, lam_table), (top_hbm, top_ref))
        )
    ]
    for table in tables:
        table.start()
    pl.semaphore_wait(barrier, 1 + above.astype(jnp.int32) + below.astype(jnp.int32) + near_across)

    for table in tables:
        table.wait()
    first_sends(0)
    prepare(0, 0)
    clear()
    relay(0, 0)
    first_sends(1)
    prepare(0, 1)
    early(0, 0)
    late(0, 0)
    water(0, 0)
    energy(0, 0)
    relay(0, 1)
    send_own(message(1, 0, 0))
    send_own(message(1, 0, 1))
    prepare(1, 0)
    early(0, 1)
    late(0, 1)
    relay(1, 0, (0,))
    solve(0, 1, True)
    relay(1, 0, (1,))
    prepare(1, 1)
    early(1, 0)
    relay(1, 1)
    late(1, 0)
    solve(1, 0)
    for field in range(2):
        for block in range(BLOCKS):
            store(0, field, block).start()
    early(1, 1)
    late(1, 1)
    solve(1, 1)
    for field in range(2):
        for block in range(BLOCKS):
            store(1, field, block).start()
    for kind in range(COPIES):

        def action(kind=kind):
            for index in range(MESSAGES):
                copy(kind, index).wait_send()

        guarded(sends[kind], action)
    for half in range(HALVES):
        for field in range(2):
            for block in range(BLOCKS):
                store(half, field, block).wait()


def solution(mesh):
    devices = mesh.shape["cols"]

    def on_device(head, warmth, kinds, top, couplings, k_sat, heat_cond):
        plane = (BLOCKS, ROWS, LANES)
        anywhere = pl.BlockSpec(memory_space=pl.ANY)
        hbm = pl.BlockSpec(memory_space=pltpu.HBM)
        f32 = jnp.float32
        out = jax.ShapeDtypeStruct(head.shape, f32)
        return pl.pallas_call(
            functools.partial(kernel, devices),
            out_shape=(out, out),
            in_specs=[hbm] * 7,
            out_specs=(anywhere, anywhere),
            scratch_shapes=[
                pltpu.VMEM((3, MESSAGES) + plane, f32),
                pltpu.VMEM((SLOTS, MESSAGES) + plane, f32),
                pltpu.VMEM((MESSAGES, ROWS, LANES), f32),
                pltpu.VMEM((HALVES, 2) + plane, f32),
                pltpu.VMEM((HALVES,) + plane, jnp.int32),
                pltpu.VMEM((HALVES,) + plane, f32),
                pltpu.VMEM((2, HALVES) + plane, f32),
                pltpu.VMEM((HALVES,) + plane, f32),
                pltpu.VMEM((HALVES,) + plane, f32),
                pltpu.VMEM((HALVES,) + plane, f32),
                pltpu.VMEM((HALVES,) + plane, f32),
                pltpu.VMEM((HALVES,) + plane, f32),
                pltpu.VMEM((CHUNK, BLOCKS, 8, LANES), f32),
                pltpu.VMEM((CHUNK, BLOCKS, 8, LANES), f32),
                pltpu.VMEM((CHUNK, BLOCKS, 8, LANES), f32),
                pltpu.VMEM((BLOCKS * HALVES, LANES), f32),
                pltpu.SMEM(couplings.shape, jnp.int32),
                pltpu.SMEM(k_sat.shape, f32),
                pltpu.SMEM(heat_cond.shape, f32),
                pltpu.SemaphoreType.DMA((4,)),
                pltpu.SemaphoreType.DMA((HALVES, 3, BLOCKS)),
                pltpu.SemaphoreType.DMA((HALVES, 2, BLOCKS)),
                pltpu.SemaphoreType.DMA((COPIES, MESSAGES)),
                pltpu.SemaphoreType.DMA((COPIES, MESSAGES)),
            ],
            compiler_params=pltpu.CompilerParams(
                collective_id=0, has_side_effects=True, vmem_limit_bytes=67043328
            ),
        )(head, warmth, kinds, top.reshape(BLOCKS * HALVES, LANES), couplings, k_sat, heat_cond)

    placed = (P(None, "cols"), P(None, "cols"), P(None, "cols"), P("cols"), P(), P(), P())
    return jax.shard_map(
        on_device,
        mesh=mesh,
        in_specs=placed,
        out_specs=(P(None, "cols"), P(None, "cols")),
        check_vma=False,
    )
```

```python
import functools

import jax
import jax.numpy as jnp
from jax import lax
from jax.experimental import pallas as pl
from jax.experimental.pallas import tpu as pltpu
from jax.sharding import PartitionSpec as P

MESH = pl.DeviceIdType.MESH

SPAN = 256
LANES = 128
HALVES = SPAN // LANES
BLOCKS = 2
ROWS = 128
CHUNK = 16
PAIR_DEV = 4

W, P1, M1, P1X, M1X, P2, M2, X2 = range(8)
SLOTS = 8
P1B, M1B = 8, 9
COPIES = 10
NATURAL, UPWARD, DOWNWARD = range(3)
MESSAGES = 10


def sig(v):
    return 1.0 / (1.0 + jnp.exp(-v))


def message(step, half, field):
    return half * 3 + field if step == 0 else 6 + half * 2 + field


def lookup(table, classes):
    result = jnp.full(classes.shape, table[0], jnp.float32)
    for entry in range(1, table.shape[0]):
        result = jnp.where(classes == entry, table[entry], result)
    return result


def down(value):
    return pltpu.roll(value, 1, 1)


def up(value):
    return pltpu.roll(value, 7, 1)


def strided(row):
    return pl.ds(row, 8, stride=CHUNK)


def forward_row(row, coef, main, above, below, source, carry):
    c_ref, a_ref, d_ref = coef
    c_prev, a_prev, d_prev = carry
    inverse = 1.0 / (main + above * c_prev)
    c_new = -below * inverse
    a_new = above * a_prev * inverse
    d_new = (source + above * d_prev) * inverse
    c_ref[row] = c_new
    a_ref[row] = a_new
    d_ref[row] = d_new
    return c_new, a_new, d_new


def finish(coef, last, write):
    c_ref, a_ref, d_ref = coef
    c_last, a_last, d_last = last
    zero = jnp.zeros_like(c_last)

    def gather(step, carry):
        d_sum, a_sum, g_sum = carry
        row = CHUNK - 2 - step
        c_row = c_ref[row]
        return d_ref[row] - c_row * d_sum, a_ref[row] - c_row * a_sum, -c_row * g_sum

    d_sum, a_sum, g_sum = lax.fori_loop(0, CHUNK - 1, gather, (zero, zero, zero - 1.0), unroll=True)
    inverse = 1.0 / (1.0 - c_last * up(a_sum))
    alpha = a_last * inverse
    gamma = -c_last * up(g_sum) * inverse
    delta = (d_last - c_last * up(d_sum)) * inverse
    for shift in (1, 2, 4):
        back = functools.partial(pltpu.roll, shift=shift, axis=1)
        ahead = functools.partial(pltpu.roll, shift=8 - shift, axis=1)
        inverse = 1.0 / (1.0 - alpha * back(gamma) - gamma * ahead(alpha))
        delta = (delta - alpha * back(delta) - gamma * ahead(delta)) * inverse
        if shift < 4:
            alpha, gamma = -alpha * back(alpha) * inverse, -gamma * ahead(gamma) * inverse
    before = down(delta)
    write(CHUNK - 1, delta)

    def back_row(step, later):
        row = CHUNK - 2 - step
        value = (d_ref[row] - a_ref[row] * before) - c_ref[row] * later
        write(row, value)
        return value

    lax.fori_loop(0, CHUNK - 1, back_row, delta, unroll=True)


def kernel(
    devices,
    head_hbm,
    warmth_hbm,
    class_hbm,
    top_hbm,
    couplings_hbm,
    k_hbm,
    lam_hbm,
    base_out,
    change_out,
    own,
    rx,
    passed,
    result,
    classes,
    lam,
    sat,
    melt,
    cond,
    energy_old,
    lat_water,
    lat_heat,
    c_ref,
    a_ref,
    d_ref,
    top_ref,
    couplings,
    k_table,
    lam_table,
    table_sem,
    load_sem,
    store_sem,
    base_sem,
    send_sem,
    recv_sem,
):
    me = lax.axis_index("cols")
    core = lax.rem(me, 2)
    other = me + 1 - 2 * core
    ahead = lax.rem(me + 2, devices)
    behind = lax.rem(me + devices - 2, devices)
    across = lax.rem(me + devices - 1 + 2 * core, devices)
    chips = devices // 2
    chip = me // 2
    coef = (c_ref, a_ref, d_ref)

    def columns(half, block):
        return pl.ds(block * SPAN + half * LANES, LANES)

    def load(half, field, block):
        source = (head_hbm, warmth_hbm, class_hbm)[field]
        target = classes.at[half, block] if field == 2 else own.at[NATURAL, message(0, half, field), block]
        return pltpu.make_async_copy(
            source.at[:, columns(half, block)], target, load_sem.at[half, field, block]
        )

    def store(half, field, block):
        return pltpu.make_async_copy(
            result.at[half, field, block],
            change_out.at[field, :, columns(half, block)],
            store_sem.at[half, field, block],
        )

    def store_base(half, field, block):
        return pltpu.make_async_copy(
            own.at[NATURAL, message(1, half, field), block],
            base_out.at[field, :, columns(half, block)],
            base_sem.at[half, field, block],
        )

    def copy(kind, index):
        if kind == W:
            source, target, device = own.at[NATURAL, index], rx.at[W, index], other
        elif kind in (P1, P1B):
            block = int(kind == P1B)
            source, target, device = own.at[UPWARD, index, block], rx.at[P1, index, block], ahead
        elif kind in (M1, M1B):
            block = int(kind == M1B)
            source, target, device = own.at[DOWNWARD, index, block], rx.at[M1, index, block], behind
        elif kind == P1X:
            source, target, device = rx.at[P1, index], rx.at[P1X, index], other
        elif kind == M1X:
            source, target, device = rx.at[M1, index], rx.at[M1X, index], other
        elif kind == P2:
            source, target, device = rx.at[P1, index, 0], rx.at[P2, index, 0], ahead
        elif kind == M2:
            source, target, device = rx.at[M1, index, 0], rx.at[M2, index, 0], behind
        else:
            source, target, device = passed.at[index], rx.at[X2, index, 0], across
        return pltpu.make_async_remote_copy(
            src_ref=source,
            dst_ref=target,
            send_sem=send_sem.at[kind, index],
            recv_sem=recv_sem.at[kind, index],
            device_id=(device,),
            device_id_type=MESH,
        )

    far_across = core * (chip <= chips - 3) + (1 - core) * (chip >= 2)
    near_across = core * (chip <= chips - 2) + (1 - core) * (chip >= 1)
    below, above = chip >= 1, chip <= chips - 2
    middle = jnp.logical_and(below, above)
    sends = {
        W: None, P1: above, P1B: above, M1: below, M1B: below, P1X: below, M1X: above,
        P2: middle, M2: middle, X2: middle,
    }
    receives = {
        W: None, P1: below, P1B: below, M1: above, M1B: above, P1X: below, M1X: above,
        P2: chip >= 2, M2: chip <= chips - 3, X2: far_across == 1,
    }

    def guarded(condition, action):
        if condition is None:
            action()
        else:
            pl.when(condition)(action)

    def start(kind, *indices):
        def action():
            for index in indices:
                copy(kind, index).start()

        guarded(sends[kind], action)

    def arrive(kind, *indices):
        def action():
            for index in indices:
                copy(kind, index).wait_recv()

        guarded(receives[kind], action)

    def order_of(device, side):
        first = device if side == 0 else lax.max(device - 4, 0)
        return couplings[side, first * PAIR_DEV + 3]

    def mask(value):
        return jnp.full((8, LANES), value, jnp.int32) == 1

    def order(index):
        swaps = [(UPWARD, mask(order_of(me, 0))), (DOWNWARD, mask(order_of(me, 1)))]

        def body(tile, carry):
            rows = pl.ds(pl.multiple_of(tile * 8, 8), 8)
            zeroth = own[NATURAL, index, 0, rows, :]
            oneth = own[NATURAL, index, 1, rows, :]
            for version, swap in swaps:
                own[version, index, 0, rows, :] = jnp.where(swap, oneth, zeroth)
                own[version, index, 1, rows, :] = jnp.where(swap, zeroth, oneth)
            return carry

        lax.fori_loop(0, ROWS // 8, body, 0, unroll=4)

    def passing(index):
        sender = lax.min(lax.max(me + 2 - 4 * core, 0), devices - 1)
        first = lax.max(sender - 3 * (1 - core), 0)
        swap = core * order_of(sender, 0) + (1 - core) * order_of(sender, 1)
        chosen = couplings[1 - core, first * PAIR_DEV + 2] + swap
        chosen = mask(chosen)
        slot = M1 - core * (M1 - P1)

        def body(tile, carry):
            rows = pl.ds(pl.multiple_of(tile * 8, 8), 8)
            passed[index, rows, :] = jnp.where(chosen, rx[slot, index, 1, rows, :], rx[slot, index, 0, rows, :])
            return carry

        lax.fori_loop(0, ROWS // 8, body, 0, unroll=4)

    def clear():
        missing = (
            (chip < 1, (P1, P1X)), (chip < 2, (P2,)), (chip > chips - 2, (M1, M1X)), (chip > chips - 3, (M2,)),
            (far_across == 0, (X2,)),
        )
        for condition, slots in missing:

            def action(slots=slots):
                def body(index, carry):
                    for slot in slots:
                        rx[slot, index] = jnp.zeros((BLOCKS, ROWS, LANES), jnp.float32)
                    return carry

                lax.fori_loop(0, MESSAGES, body, 0)

            pl.when(condition)(action)

    def lookups(half):
        def body(tile, carry):
            rows = pl.ds(pl.multiple_of(tile * 8, 8), 8)
            for block in range(BLOCKS):
                kinds = classes[half, block, rows, :]
                own[NATURAL, message(0, half, 2), block, rows, :] = lookup(k_table, kinds)
                lam[half, block, rows, :] = lookup(lam_table, kinds)
            return carry

        lax.fori_loop(0, ROWS // 8, body, 0)

    def prepare(step, half):
        def body(tile, carry):
            rows = pl.ds(pl.multiple_of(tile * 8, 8), 8)
            for block in range(BLOCKS):
                head = own[NATURAL, message(step, half, 0), block, rows, :]
                warmth = own[NATURAL, message(step, half, 1), block, rows, :]
                filled = sig(head)
                liquid = sig(2.0 * warmth)
                sat[step, half, block, rows, :] = filled
                melt[half, block, rows, :] = liquid
                cond[half, block, rows, :] = own[NATURAL, message(0, half, 2), block, rows, :] * (
                    liquid * filled * filled + 0.02
                )
                if step == 0:
                    moist = 0.05 + 0.4 * filled
                    energy_old[half, block, rows, :] = (
                        1.0 + 2.0 * moist
                    ) * warmth + 2.0 * moist * liquid
            return carry

        lax.fori_loop(0, ROWS // 8, body, 0)

    def pair_of(slot):
        upper = {M1: 1, M1X: 1, M2: 1, P1: 0, P1X: 0, P2: 0, W: 1 - core, X2: core}[slot]
        distance = {
            M1: 2, P1: 2, M2: 4, P2: 4, W: 1, X2: 3, M1X: 3 - 2 * core, P1X: 1 + 2 * core
        }[slot]
        sender = me + (2 * upper - 1) * distance
        first = me - (1 - upper) * distance
        valid = jnp.logical_and(first >= 0, first + distance < devices).astype(jnp.int32)
        pair = lax.rem(first + devices, devices) * PAIR_DEV + distance - 1
        sender = lax.min(lax.max(sender, 0), devices - 1)
        swap = order_of(sender, upper) if isinstance(upper, int) else 0
        return upper, pair, valid, swap

    def lateral(step, half, slots, first):
        settings = []
        for slot in slots:
            upper, pair, valid, swap = pair_of(slot)
            mine = couplings[1 - upper, pair]
            theirs = couplings[upper, pair] + swap
            slope = jnp.full((8, LANES), upper.astype(jnp.float32) - 0.5 if not isinstance(upper, int) else upper - 0.5)
            settings.append((slot, slope, mask(mine), mask(theirs), mask(valid)))

        def body(tile, carry):
            rows = pl.ds(pl.multiple_of(tile * 8, 8), 8)
            heads = [own[NATURAL, message(step, half, 0), block, rows, :] for block in range(BLOCKS)]
            warmths = [own[NATURAL, message(step, half, 1), block, rows, :] for block in range(BLOCKS)]
            conds = [cond[half, block, rows, :] for block in range(BLOCKS)]
            zero = jnp.zeros((8, LANES), jnp.float32)
            if first:
                water = [zero, zero]
                heat = [zero, zero]
            else:
                water = [lat_water[half, block, rows, :] for block in range(BLOCKS)]
                heat = [lat_heat[half, block, rows, :] for block in range(BLOCKS)]
            for slot, slope, mine, theirs, live in settings:

                def far(field, at):
                    index = message(at, half, field)
                    if slot in (P2, M2, X2):
                        return rx[slot, index, 0, rows, :]
                    return jnp.where(theirs, rx[slot, index, 1, rows, :], rx[slot, index, 0, rows, :])

                far_head, far_warmth, far_k = far(0, step), far(1, step), far(2, 0)
                filled = sig(far_head)
                far_cond = far_k * (sig(2.0 * far_warmth) * filled * filled + 0.02)
                near_head = jnp.where(mine, heads[1], heads[0])
                near_warmth = jnp.where(mine, warmths[1], warmths[0])
                near_cond = jnp.where(mine, conds[1], conds[0])
                flow = 0.25 * (near_cond + far_cond) * (near_head - far_head + slope)
                flow = jnp.where(live, flow, 0.0)
                carried = 2.0 * (
                    jnp.maximum(flow, 0.0) * near_warmth + jnp.minimum(flow, 0.0) * far_warmth
                )
                water[0] = water[0] - jnp.where(mine, 0.0, flow)
                water[1] = water[1] - jnp.where(mine, flow, 0.0)
                heat[0] = heat[0] - jnp.where(mine, 0.0, carried)
                heat[1] = heat[1] - jnp.where(mine, carried, 0.0)
            for block in range(BLOCKS):
                lat_water[half, block, rows, :] = water[block]
                lat_heat[half, block, rows, :] = heat[block]
            return carry

        lax.fori_loop(0, ROWS // 8, body, 0)

    sublane = lax.broadcasted_iota(jnp.int32, (BLOCKS, 8, LANES), 1)
    is_top = sublane == 0

    def new_head(step, half, row):
        if step == 0:
            return own[NATURAL, message(1, half, 0), :, strided(row), :]
        return own[NATURAL, message(1, half, 0), :, strided(row), :] + result[half, 0, :, strided(row), :]

    def water(step, half):
        index = message(step, half, 0)

        def cond_row(row):
            return cond[half, :, strided(row), :]

        def head_row(row):
            return own[NATURAL, index, :, strided(row), :]

        def one(row, k_above, q_above, k_below, q_below, carry):
            filled = sat[step, half, :, strided(row), :]
            source = lat_water[half, :, strided(row), :] + q_above - q_below
            if step > 0:
                source = source - 0.8 * (filled - sat[0, half, :, strided(row), :])
            main = 0.8 * filled * (1.0 - filled) + 0.02 + k_above + k_below
            return forward_row(row, coef, main, k_above, k_below, source, carry)

        zero = jnp.zeros((BLOCKS, 8, LANES), jnp.float32)
        cond_first, head_first = cond_row(0), head_row(0)
        k_first = jnp.where(is_top, 0.0, 0.5 * (down(cond_row(CHUNK - 1)) + cond_first))
        q_first = -k_first * (head_first - down(head_row(CHUNK - 1)) - 1.0)

        def body(row, carry):
            cond_here, head_here, k_above, q_above, *chain = carry
            cond_next, head_next = cond_row(row + 1), head_row(row + 1)
            k_below = 0.5 * (cond_here + cond_next)
            q_below = -k_below * (head_next - head_here - 1.0)
            chain = one(row, k_above, q_above, k_below, q_below, chain)
            return (cond_next, head_next, k_below, q_below, *chain)

        start = (cond_first, head_first, k_first, q_first, zero, zero - 1.0, zero)
        _, _, k_above, q_above, *chain = lax.fori_loop(0, CHUNK - 1, body, start, unroll=True)
        last = one(CHUNK - 1, k_above, q_above, up(k_first), up(q_first), chain)

        def write(row, change):
            if step == 0:
                own[NATURAL, message(1, half, 0), :, strided(row), :] = head_row(row) + change
            else:
                result[half, 0, :, strided(row), :] = change

        finish(coef, last, write)

    def energy(step, half):
        index = message(step, half, 1)

        def warmth_row(row):
            return own[NATURAL, index, :, strided(row), :]

        def passing_row(row):
            return lam[half, :, strided(row), :] * (1.5 - 0.5 * melt[half, :, strided(row), :])

        def one(row, here, extra, k_above, q_above, k_below, q_below, carry):
            moist = 0.05 + 0.4 * sig(new_head(step, half, row))
            liquid = melt[half, :, strided(row), :]
            slack = 1.0 + 2.0 * moist
            stored = slack * here + 2.0 * moist * liquid
            source = (
                lat_heat[half, :, strided(row), :]
                + q_above
                - q_below
                - 2.0 * (stored - energy_old[half, :, strided(row), :])
            )
            main = 2.0 * (slack + 4.0 * moist * liquid * (1.0 - liquid)) + k_above + k_below
            if extra is not None:
                main = main + extra
            return forward_row(row, coef, main, k_above, k_below, source, carry)

        zero = jnp.zeros((BLOCKS, 8, LANES), jnp.float32)
        passing_first, warmth_first = passing_row(0), warmth_row(0)
        top = jnp.stack(
            [
                jnp.broadcast_to(top_ref[pl.ds(block * HALVES + half, 1), :], (8, LANES))
                for block in range(BLOCKS)
            ]
        )
        k_first = jnp.where(is_top, 0.0, 0.5 * (down(passing_row(CHUNK - 1)) + passing_first))
        q_first = -k_first * (warmth_first - down(warmth_row(CHUNK - 1)))
        surface = jnp.where(is_top, 2.0 * passing_first, 0.0)
        q_surface = q_first + surface * (top - warmth_first)

        def body(row, carry):
            passing_here, warmth_here, extra, k_above, q_above, *chain = carry
            passing_next, warmth_next = passing_row(row + 1), warmth_row(row + 1)
            k_below = 0.5 * (passing_here + passing_next)
            q_below = -k_below * (warmth_next - warmth_here)
            chain = one(row, warmth_here, extra, k_above, q_above, k_below, q_below, chain)
            return (passing_next, warmth_next, zero, k_below, q_below, *chain)

        start = (passing_first, warmth_first, surface, k_first, q_surface, zero, zero - 1.0, zero)
        _, here, _, k_above, q_above, *chain = lax.fori_loop(0, CHUNK - 1, body, start, unroll=True)
        last = one(CHUNK - 1, here, None, k_above, q_above, up(k_first), up(q_first), chain)

        def write(row, change):
            if step == 0:
                own[NATURAL, message(1, half, 1), :, strided(row), :] = warmth_row(row) + change
            else:
                result[half, 1, :, strided(row), :] = change

        finish(coef, last, write)

    def send_own(index):
        start(W, index)
        order(index)
        start(P1, index)
        start(M1, index)
        start(P1B, index)
        start(M1B, index)

    def first_sends(half):
        for field in range(2):
            for block in range(BLOCKS):
                load(half, field, block).wait()
            send_own(message(0, half, field))
        for block in range(BLOCKS):
            load(half, 2, block).wait()
        lookups(half)
        send_own(message(0, half, 2))

    def indices_of(step, half):
        return [message(step, half, field) for field in range(3 if step == 0 else 2)]

    def relay(step, half, fields=(0, 1, 2)):
        for index in [message(step, half, field) for field in fields if step == 0 or field < 2]:
            arrive(P1, index)
            start(P2, index)
            arrive(M1, index)
            start(M2, index)
            arrive(P1B, index)
            arrive(M1B, index)
            passing(index)
            start(P1X, index)
            start(M1X, index)
            start(X2, index)

    def early(step, half):
        arrive(W, *indices_of(step, half))
        lateral(step, half, (W, P1, M1), True)

    def late(step, half):
        indices = indices_of(step, half)
        arrive(P1X, *indices)
        arrive(M1X, *indices)
        lateral(step, half, (P1X, M1X), False)
        arrive(P2, *indices)
        arrive(M2, *indices)
        lateral(step, half, (P2, M2), False)
        arrive(X2, *indices)
        lateral(step, half, (X2,), False)

    def solve(step, half, send=False):
        water(step, half)
        if send:
            send_own(message(1, half, 0))
        energy(step, half)
        if send:
            send_own(message(1, half, 1))

    barrier = pltpu.get_barrier_semaphore()
    pl.semaphore_signal(barrier, inc=1, device_id=(other,), device_id_type=MESH)

    @pl.when(above)
    def _():
        pl.semaphore_signal(barrier, inc=1, device_id=(ahead,), device_id_type=MESH)

    @pl.when(below)
    def _():
        pl.semaphore_signal(barrier, inc=1, device_id=(behind,), device_id_type=MESH)

    @pl.when(near_across == 1)
    def _():
        pl.semaphore_signal(barrier, inc=1, device_id=(across,), device_id_type=MESH)

    tables = [
        pltpu.make_async_copy(source, target, table_sem.at[place])
        for place, (source, target) in enumerate(
            ((couplings_hbm, couplings), (k_hbm, k_table), (lam_hbm, lam_table), (top_hbm, top_ref))
        )
    ]
    tables[0].start()
    for half in range(HALVES):
        for field in range(3):
            for block in range(BLOCKS):
                load(half, field, block).start()
    for table in tables[1:]:
        table.start()
    pl.semaphore_wait(barrier, 1 + above.astype(jnp.int32) + below.astype(jnp.int32) + near_across)

    for table in tables:
        table.wait()
    first_sends(0)
    prepare(0, 0)
    clear()
    relay(0, 0)
    first_sends(1)
    prepare(0, 1)
    early(0, 0)
    late(0, 0)
    water(0, 0)
    energy(0, 0)
    relay(0, 1)
    send_own(message(1, 0, 0))
    send_own(message(1, 0, 1))
    prepare(1, 0)
    early(0, 1)
    late(0, 1)
    relay(1, 0, (0,))
    solve(0, 1, True)
    relay(1, 0, (1,))
    prepare(1, 1)
    early(1, 0)
    relay(1, 1)
    early(1, 1)
    late(1, 0)
    solve(1, 0)
    for field in range(2):
        for block in range(BLOCKS):
            store(0, field, block).start()
            for half in range(HALVES):
                store_base(half, field, block).start()
    late(1, 1)
    solve(1, 1)
    for field in range(2):
        for block in range(BLOCKS):
            store(1, field, block).start()
    for kind in range(COPIES):

        def action(kind=kind):
            for index in range(MESSAGES):
                copy(kind, index).wait_send()

        guarded(sends[kind], action)
    for half in range(HALVES):
        for field in range(2):
            for block in range(BLOCKS):
                store(half, field, block).wait()
                store_base(half, field, block).wait()


def solution(mesh):
    devices = mesh.shape["cols"]

    def on_device(head, warmth, kinds, top, couplings, k_sat, heat_cond):
        plane = (BLOCKS, ROWS, LANES)
        hbm = pl.BlockSpec(memory_space=pltpu.HBM)
        f32 = jnp.float32
        out = pltpu.VMEM((2,) + head.shape, f32)
        base, change = pl.pallas_call(
            functools.partial(kernel, devices),
            out_shape=(out, out),
            in_specs=[hbm] * 7,
            out_specs=(pl.BlockSpec(memory_space=pltpu.VMEM),) * 2,
            scratch_shapes=[
                pltpu.VMEM((3, MESSAGES) + plane, f32),
                pltpu.VMEM((SLOTS, MESSAGES) + plane, f32),
                pltpu.VMEM((MESSAGES, ROWS, LANES), f32),
                pltpu.VMEM((HALVES, 2) + plane, f32),
                pltpu.VMEM((HALVES,) + plane, jnp.int32),
                pltpu.VMEM((HALVES,) + plane, f32),
                pltpu.VMEM((2, HALVES) + plane, f32),
                pltpu.VMEM((HALVES,) + plane, f32),
                pltpu.VMEM((HALVES,) + plane, f32),
                pltpu.VMEM((HALVES,) + plane, f32),
                pltpu.VMEM((HALVES,) + plane, f32),
                pltpu.VMEM((HALVES,) + plane, f32),
                pltpu.VMEM((CHUNK, BLOCKS, 8, LANES), f32),
                pltpu.VMEM((CHUNK, BLOCKS, 8, LANES), f32),
                pltpu.VMEM((CHUNK, BLOCKS, 8, LANES), f32),
                pltpu.VMEM((BLOCKS * HALVES, LANES), f32),
                pltpu.SMEM(couplings.shape, jnp.int32),
                pltpu.SMEM(k_sat.shape, f32),
                pltpu.SMEM(heat_cond.shape, f32),
                pltpu.SemaphoreType.DMA((4,)),
                pltpu.SemaphoreType.DMA((HALVES, 3, BLOCKS)),
                pltpu.SemaphoreType.DMA((HALVES, 2, BLOCKS)),
                pltpu.SemaphoreType.DMA((HALVES, 2, BLOCKS)),
                pltpu.SemaphoreType.DMA((COPIES, MESSAGES)),
                pltpu.SemaphoreType.DMA((COPIES, MESSAGES)),
            ],
            compiler_params=pltpu.CompilerParams(
                collective_id=0, has_side_effects=True, vmem_limit_bytes=65900000
            ),
        )(head, warmth, kinds, top.reshape(BLOCKS * HALVES, LANES), couplings, k_sat, heat_cond)
        return base[0] + change[0], base[1] + change[1]

    placed = (P(None, "cols"), P(None, "cols"), P(None, "cols"), P("cols"), P(), P(), P())
    return jax.shard_map(
        on_device,
        mesh=mesh,
        in_specs=placed,
        out_specs=(P(None, "cols"), P(None, "cols")),
        check_vma=False,
    )
```

```python
import functools

import jax
import jax.numpy as jnp
from jax import lax
from jax.experimental import pallas as pl
from jax.experimental.pallas import tpu as pltpu
from jax.sharding import PartitionSpec as P

MESH = pl.DeviceIdType.MESH

SPAN = 256
LANES = 128
HALVES = SPAN // LANES
BLOCKS = 2
ROWS = 128
CHUNK = 16
PAIR_DEV = 4

W, P1, M1, P1X, M1X, P2, M2, X2 = range(8)
SLOTS = 8
P1B, M1B = 8, 9
COPIES = 10
SINGLE = (P1, P1B, M1, M1B)
GROUPED = (W, P1X, M1X, P2, M2, X2)
NATURAL, UPWARD, DOWNWARD = range(3)
MESSAGES = 10


def sig(v):
    return 1.0 / (1.0 + jnp.exp(-v))


def message(step, half, field):
    return half * 3 + field if step == 0 else 6 + half * 2 + field


def lookup(table, classes):
    result = jnp.full(classes.shape, table[0], jnp.float32)
    for entry in range(1, table.shape[0]):
        result = jnp.where(classes == entry, table[entry], result)
    return result


def down(value):
    return pltpu.roll(value, 1, 1)


def up(value):
    return pltpu.roll(value, 7, 1)


def strided(row):
    return pl.ds(row, 8, stride=CHUNK)


def forward_row(row, coef, main, above, below, source, carry):
    c_ref, a_ref, d_ref = coef
    c_prev, a_prev, d_prev = carry
    inverse = 1.0 / (main + above * c_prev)
    c_new = -below * inverse
    a_new = above * a_prev * inverse
    d_new = (source + above * d_prev) * inverse
    c_ref[row] = c_new
    a_ref[row] = a_new
    d_ref[row] = d_new
    return c_new, a_new, d_new


def finish(coef, last, write):
    c_ref, a_ref, d_ref = coef
    c_last, a_last, d_last = last
    zero = jnp.zeros_like(c_last)

    def gather(step, carry):
        d_sum, a_sum, g_sum = carry
        row = CHUNK - 2 - step
        c_row = c_ref[row]
        return d_ref[row] - c_row * d_sum, a_ref[row] - c_row * a_sum, -c_row * g_sum

    d_sum, a_sum, g_sum = lax.fori_loop(0, CHUNK - 1, gather, (zero, zero, zero - 1.0), unroll=True)
    inverse = 1.0 / (1.0 - c_last * up(a_sum))
    alpha = a_last * inverse
    gamma = -c_last * up(g_sum) * inverse
    delta = (d_last - c_last * up(d_sum)) * inverse
    for shift in (1, 2, 4):
        back = functools.partial(pltpu.roll, shift=shift, axis=1)
        ahead = functools.partial(pltpu.roll, shift=8 - shift, axis=1)
        inverse = 1.0 / (1.0 - alpha * back(gamma) - gamma * ahead(alpha))
        delta = (delta - alpha * back(delta) - gamma * ahead(delta)) * inverse
        if shift < 4:
            alpha, gamma = -alpha * back(alpha) * inverse, -gamma * ahead(gamma) * inverse
    before = down(delta)
    write(CHUNK - 1, delta)

    def back_row(step, later):
        row = CHUNK - 2 - step
        value = (d_ref[row] - a_ref[row] * before) - c_ref[row] * later
        write(row, value)
        return value

    lax.fori_loop(0, CHUNK - 1, back_row, delta, unroll=True)


def kernel(
    devices,
    head_hbm,
    warmth_hbm,
    class_hbm,
    top_hbm,
    couplings_hbm,
    k_hbm,
    lam_hbm,
    base_out,
    change_out,
    own,
    rx,
    passed,
    result,
    classes,
    lam,
    sat,
    melt,
    cond,
    energy_old,
    lat_water,
    lat_heat,
    c_ref,
    a_ref,
    d_ref,
    top_ref,
    couplings,
    k_table,
    lam_table,
    table_sem,
    load_sem,
    store_sem,
    send_sem,
    single_sem,
    group_sem,
):
    me = lax.axis_index("cols")
    core = lax.rem(me, 2)
    other = me + 1 - 2 * core
    ahead = lax.rem(me + 2, devices)
    behind = lax.rem(me + devices - 2, devices)
    across = lax.rem(me + devices - 1 + 2 * core, devices)
    chips = devices // 2
    chip = me // 2
    coef = (c_ref, a_ref, d_ref)

    def columns(half, block):
        return pl.ds(block * SPAN + half * LANES, LANES)

    def load(half, field, block):
        source = (head_hbm, warmth_hbm, class_hbm)[field]
        target = classes.at[half, block] if field == 2 else own.at[NATURAL, message(0, half, field), block]
        return pltpu.make_async_copy(
            source.at[:, columns(half, block)], target, load_sem.at[half, field]
        )

    def loaded(half, field):
        ref = classes.at[half] if field == 2 else own.at[NATURAL, message(0, half, field)]
        pltpu.make_async_copy(ref, ref, load_sem.at[half, field]).wait()

    def store(half, field, block):
        return pltpu.make_async_copy(
            result.at[half, field, block],
            change_out.at[field, :, columns(half, block)],
            store_sem.at[0],
        )

    def store_base(half, field, block):
        return pltpu.make_async_copy(
            own.at[NATURAL, message(1, half, field), block],
            base_out.at[field, :, columns(half, block)],
            store_sem.at[1],
        )

    def copy(kind, index):
        if kind == W:
            source, target, device = own.at[NATURAL, index], rx.at[W, index], other
        elif kind in (P1, P1B):
            block = int(kind == P1B)
            source, target, device = own.at[UPWARD, index, block], rx.at[P1, index, block], ahead
        elif kind in (M1, M1B):
            block = int(kind == M1B)
            source, target, device = own.at[DOWNWARD, index, block], rx.at[M1, index, block], behind
        elif kind == P1X:
            source, target, device = rx.at[P1, index], rx.at[P1X, index], other
        elif kind == M1X:
            source, target, device = rx.at[M1, index], rx.at[M1X, index], other
        elif kind == P2:
            source, target, device = rx.at[P1, index, 0], rx.at[P2, index, 0], ahead
        elif kind == M2:
            source, target, device = rx.at[M1, index, 0], rx.at[M2, index, 0], behind
        else:
            source, target, device = passed.at[index], rx.at[X2, index, 0], across
        return pltpu.make_async_remote_copy(
            src_ref=source,
            dst_ref=target,
            send_sem=send_sem.at[kind],
            recv_sem=arrival_sem(kind, index),
            device_id=(device,),
            device_id_type=MESH,
        )

    def arrival_sem(kind, index):
        if kind in SINGLE:
            return single_sem.at[SINGLE.index(kind), index]
        return group_sem.at[GROUPED.index(kind), index // 3 if index < 6 else index // 2 - 1]

    def whole(kind, ref, arrival):
        return pltpu.make_async_remote_copy(
            src_ref=ref, dst_ref=ref, send_sem=send_sem.at[kind], recv_sem=arrival, device_id=(other,), device_id_type=MESH
        )

    far_across = core * (chip <= chips - 3) + (1 - core) * (chip >= 2)
    near_across = core * (chip <= chips - 2) + (1 - core) * (chip >= 1)
    below, above = chip >= 1, chip <= chips - 2
    middle = jnp.logical_and(below, above)
    sends = {
        W: None, P1: above, P1B: above, M1: below, M1B: below, P1X: below, M1X: above,
        P2: middle, M2: middle, X2: middle,
    }
    receives = {
        W: None, P1: below, P1B: below, M1: above, M1B: above, P1X: below, M1X: above,
        P2: chip >= 2, M2: chip <= chips - 3, X2: far_across == 1,
    }

    def guarded(condition, action):
        if condition is None:
            action()
        else:
            pl.when(condition)(action)

    def start(kind, *indices):
        def action():
            for index in indices:
                copy(kind, index).start()

        guarded(sends[kind], action)

    def arrive(kind, *indices):
        def action():
            if kind in SINGLE:
                for index in indices:
                    copy(kind, index).wait_recv()
            else:
                span = pl.ds(indices[0], len(indices))
                ref = rx.at[kind, span] if kind in (W, P1X, M1X) else rx.at[kind, span, 0]
                whole(kind, ref, arrival_sem(kind, indices[0])).wait_recv()

        guarded(receives[kind], action)

    def order_of(device, side):
        first = device if side == 0 else lax.max(device - 4, 0)
        return couplings[side, first * PAIR_DEV + 3]

    def mask(value):
        return jnp.full((8, LANES), value, jnp.int32) == 1

    def order(index):
        swaps = [(UPWARD, mask(order_of(me, 0))), (DOWNWARD, mask(order_of(me, 1)))]

        def body(tile, carry):
            rows = pl.ds(pl.multiple_of(tile * 8, 8), 8)
            zeroth = own[NATURAL, index, 0, rows, :]
            oneth = own[NATURAL, index, 1, rows, :]
            for version, swap in swaps:
                own[version, index, 0, rows, :] = jnp.where(swap, oneth, zeroth)
                own[version, index, 1, rows, :] = jnp.where(swap, zeroth, oneth)
            return carry

        lax.fori_loop(0, ROWS // 8, body, 0, unroll=4)

    def passing(index):
        sender = lax.min(lax.max(me + 2 - 4 * core, 0), devices - 1)
        first = lax.max(sender - 3 * (1 - core), 0)
        swap = core * order_of(sender, 0) + (1 - core) * order_of(sender, 1)
        chosen = couplings[1 - core, first * PAIR_DEV + 2] + swap
        chosen = mask(chosen)
        slot = M1 - core * (M1 - P1)

        def body(tile, carry):
            rows = pl.ds(pl.multiple_of(tile * 8, 8), 8)
            passed[index, rows, :] = jnp.where(chosen, rx[slot, index, 1, rows, :], rx[slot, index, 0, rows, :])
            return carry

        lax.fori_loop(0, ROWS // 8, body, 0, unroll=4)

    def clear():
        missing = (
            (chip < 1, (P1, P1X)), (chip < 2, (P2,)), (chip > chips - 2, (M1, M1X)), (chip > chips - 3, (M2,)),
            (far_across == 0, (X2,)),
        )
        for condition, slots in missing:

            def action(slots=slots):
                def body(index, carry):
                    for slot in slots:
                        rx[slot, index] = jnp.zeros((BLOCKS, ROWS, LANES), jnp.float32)
                    return carry

                lax.fori_loop(0, MESSAGES, body, 0)

            pl.when(condition)(action)

    def lookups(half):
        def body(tile, carry):
            rows = pl.ds(pl.multiple_of(tile * 8, 8), 8)
            for block in range(BLOCKS):
                kinds = classes[half, block, rows, :]
                own[NATURAL, message(0, half, 2), block, rows, :] = lookup(k_table, kinds)
                lam[half, block, rows, :] = lookup(lam_table, kinds)
            return carry

        lax.fori_loop(0, ROWS // 8, body, 0)

    def prepare(step, half):
        def body(tile, carry):
            rows = pl.ds(pl.multiple_of(tile * 8, 8), 8)
            for block in range(BLOCKS):
                head = own[NATURAL, message(step, half, 0), block, rows, :]
                warmth = own[NATURAL, message(step, half, 1), block, rows, :]
                filled = sig(head)
                liquid = sig(2.0 * warmth)
                sat[step, half, block, rows, :] = filled
                melt[half, block, rows, :] = liquid
                cond[half, block, rows, :] = own[NATURAL, message(0, half, 2), block, rows, :] * (
                    liquid * filled * filled + 0.02
                )
                if step == 0:
                    moist = 0.05 + 0.4 * filled
                    energy_old[half, block, rows, :] = (
                        1.0 + 2.0 * moist
                    ) * warmth + 2.0 * moist * liquid
            return carry

        lax.fori_loop(0, ROWS // 8, body, 0)

    def pair_of(slot):
        upper = {M1: 1, M1X: 1, M2: 1, P1: 0, P1X: 0, P2: 0, W: 1 - core, X2: core}[slot]
        distance = {
            M1: 2, P1: 2, M2: 4, P2: 4, W: 1, X2: 3, M1X: 3 - 2 * core, P1X: 1 + 2 * core
        }[slot]
        sender = me + (2 * upper - 1) * distance
        first = me - (1 - upper) * distance
        valid = jnp.logical_and(first >= 0, first + distance < devices).astype(jnp.int32)
        pair = lax.rem(first + devices, devices) * PAIR_DEV + distance - 1
        sender = lax.min(lax.max(sender, 0), devices - 1)
        swap = order_of(sender, upper) if isinstance(upper, int) else 0
        return upper, pair, valid, swap

    def lateral(step, half, slots, first):
        settings = []
        for slot in slots:
            upper, pair, valid, swap = pair_of(slot)
            mine = couplings[1 - upper, pair]
            theirs = couplings[upper, pair] + swap
            slope = jnp.full((8, LANES), upper.astype(jnp.float32) - 0.5 if not isinstance(upper, int) else upper - 0.5)
            settings.append((slot, slope, mask(mine), mask(theirs), mask(valid)))

        def body(tile, carry):
            rows = pl.ds(pl.multiple_of(tile * 8, 8), 8)
            heads = [own[NATURAL, message(step, half, 0), block, rows, :] for block in range(BLOCKS)]
            warmths = [own[NATURAL, message(step, half, 1), block, rows, :] for block in range(BLOCKS)]
            conds = [cond[half, block, rows, :] for block in range(BLOCKS)]
            zero = jnp.zeros((8, LANES), jnp.float32)
            if first:
                water = [zero, zero]
                heat = [zero, zero]
            else:
                water = [lat_water[half, block, rows, :] for block in range(BLOCKS)]
                heat = [lat_heat[half, block, rows, :] for block in range(BLOCKS)]
            for slot, slope, mine, theirs, live in settings:

                def far(field, at):
                    index = message(at, half, field)
                    if slot in (P2, M2, X2):
                        return rx[slot, index, 0, rows, :]
                    return jnp.where(theirs, rx[slot, index, 1, rows, :], rx[slot, index, 0, rows, :])

                far_head, far_warmth, far_k = far(0, step), far(1, step), far(2, 0)
                filled = sig(far_head)
                far_cond = far_k * (sig(2.0 * far_warmth) * filled * filled + 0.02)
                near_head = jnp.where(mine, heads[1], heads[0])
                near_warmth = jnp.where(mine, warmths[1], warmths[0])
                near_cond = jnp.where(mine, conds[1], conds[0])
                flow = 0.25 * (near_cond + far_cond) * (near_head - far_head + slope)
                flow = jnp.where(live, flow, 0.0)
                carried = 2.0 * (
                    jnp.maximum(flow, 0.0) * near_warmth + jnp.minimum(flow, 0.0) * far_warmth
                )
                water[0] = water[0] - jnp.where(mine, 0.0, flow)
                water[1] = water[1] - jnp.where(mine, flow, 0.0)
                heat[0] = heat[0] - jnp.where(mine, 0.0, carried)
                heat[1] = heat[1] - jnp.where(mine, carried, 0.0)
            for block in range(BLOCKS):
                lat_water[half, block, rows, :] = water[block]
                lat_heat[half, block, rows, :] = heat[block]
            return carry

        lax.fori_loop(0, ROWS // 8, body, 0)

    sublane = lax.broadcasted_iota(jnp.int32, (BLOCKS, 8, LANES), 1)
    is_top = sublane == 0

    def new_head(step, half, row):
        if step == 0:
            return own[NATURAL, message(1, half, 0), :, strided(row), :]
        return own[NATURAL, message(1, half, 0), :, strided(row), :] + result[half, 0, :, strided(row), :]

    def water(step, half):
        index = message(step, half, 0)

        def cond_row(row):
            return cond[half, :, strided(row), :]

        def head_row(row):
            return own[NATURAL, index, :, strided(row), :]

        def one(row, k_above, q_above, k_below, q_below, carry):
            filled = sat[step, half, :, strided(row), :]
            source = lat_water[half, :, strided(row), :] + q_above - q_below
            if step > 0:
                source = source - 0.8 * (filled - sat[0, half, :, strided(row), :])
            main = 0.8 * filled * (1.0 - filled) + 0.02 + k_above + k_below
            return forward_row(row, coef, main, k_above, k_below, source, carry)

        zero = jnp.zeros((BLOCKS, 8, LANES), jnp.float32)
        cond_first, head_first = cond_row(0), head_row(0)
        k_first = jnp.where(is_top, 0.0, 0.5 * (down(cond_row(CHUNK - 1)) + cond_first))
        q_first = -k_first * (head_first - down(head_row(CHUNK - 1)) - 1.0)

        def body(row, carry):
            cond_here, head_here, k_above, q_above, *chain = carry
            cond_next, head_next = cond_row(row + 1), head_row(row + 1)
            k_below = 0.5 * (cond_here + cond_next)
            q_below = -k_below * (head_next - head_here - 1.0)
            chain = one(row, k_above, q_above, k_below, q_below, chain)
            return (cond_next, head_next, k_below, q_below, *chain)

        start = (cond_first, head_first, k_first, q_first, zero, zero - 1.0, zero)
        _, _, k_above, q_above, *chain = lax.fori_loop(0, CHUNK - 1, body, start, unroll=True)
        last = one(CHUNK - 1, k_above, q_above, up(k_first), up(q_first), chain)

        def write(row, change):
            if step == 0:
                own[NATURAL, message(1, half, 0), :, strided(row), :] = head_row(row) + change
            else:
                result[half, 0, :, strided(row), :] = change

        finish(coef, last, write)

    def energy(step, half):
        index = message(step, half, 1)

        def warmth_row(row):
            return own[NATURAL, index, :, strided(row), :]

        def passing_row(row):
            return lam[half, :, strided(row), :] * (1.5 - 0.5 * melt[half, :, strided(row), :])

        def one(row, here, extra, k_above, q_above, k_below, q_below, carry):
            moist = 0.05 + 0.4 * sig(new_head(step, half, row))
            liquid = melt[half, :, strided(row), :]
            slack = 1.0 + 2.0 * moist
            stored = slack * here + 2.0 * moist * liquid
            source = (
                lat_heat[half, :, strided(row), :]
                + q_above
                - q_below
                - 2.0 * (stored - energy_old[half, :, strided(row), :])
            )
            main = 2.0 * (slack + 4.0 * moist * liquid * (1.0 - liquid)) + k_above + k_below
            if extra is not None:
                main = main + extra
            return forward_row(row, coef, main, k_above, k_below, source, carry)

        zero = jnp.zeros((BLOCKS, 8, LANES), jnp.float32)
        passing_first, warmth_first = passing_row(0), warmth_row(0)
        top = jnp.stack(
            [
                jnp.broadcast_to(top_ref[pl.ds(block * HALVES + half, 1), :], (8, LANES))
                for block in range(BLOCKS)
            ]
        )
        k_first = jnp.where(is_top, 0.0, 0.5 * (down(passing_row(CHUNK - 1)) + passing_first))
        q_first = -k_first * (warmth_first - down(warmth_row(CHUNK - 1)))
        surface = jnp.where(is_top, 2.0 * passing_first, 0.0)
        q_surface = q_first + surface * (top - warmth_first)

        def body(row, carry):
            passing_here, warmth_here, extra, k_above, q_above, *chain = carry
            passing_next, warmth_next = passing_row(row + 1), warmth_row(row + 1)
            k_below = 0.5 * (passing_here + passing_next)
            q_below = -k_below * (warmth_next - warmth_here)
            chain = one(row, warmth_here, extra, k_above, q_above, k_below, q_below, chain)
            return (passing_next, warmth_next, zero, k_below, q_below, *chain)

        start = (passing_first, warmth_first, surface, k_first, q_surface, zero, zero - 1.0, zero)
        _, here, _, k_above, q_above, *chain = lax.fori_loop(0, CHUNK - 1, body, start, unroll=True)
        last = one(CHUNK - 1, here, None, k_above, q_above, up(k_first), up(q_first), chain)

        def write(row, change):
            if step == 0:
                own[NATURAL, message(1, half, 1), :, strided(row), :] = warmth_row(row) + change
            else:
                result[half, 1, :, strided(row), :] = change

        finish(coef, last, write)

    def send_own(index):
        start(W, index)
        order(index)
        start(P1, index)
        start(M1, index)
        start(P1B, index)
        start(M1B, index)

    def first_sends(half):
        for field in range(2):
            loaded(half, field)
            send_own(message(0, half, field))
        loaded(half, 2)
        lookups(half)
        send_own(message(0, half, 2))

    def indices_of(step, half):
        return [message(step, half, field) for field in range(3 if step == 0 else 2)]

    def relay(step, half, fields=(0, 1, 2)):
        for index in [message(step, half, field) for field in fields if step == 0 or field < 2]:
            arrive(P1, index)
            start(P2, index)
            arrive(M1, index)
            start(M2, index)
            arrive(P1B, index)
            arrive(M1B, index)
            passing(index)
            start(P1X, index)
            start(M1X, index)
            start(X2, index)

    def early(step, half):
        arrive(W, *indices_of(step, half))
        lateral(step, half, (W, P1, M1), True)

    def late(step, half):
        indices = indices_of(step, half)
        arrive(P1X, *indices)
        arrive(M1X, *indices)
        lateral(step, half, (P1X, M1X), False)
        arrive(P2, *indices)
        arrive(M2, *indices)
        lateral(step, half, (P2, M2), False)
        arrive(X2, *indices)
        lateral(step, half, (X2,), False)

    def solve(step, half, send=False):
        water(step, half)
        if send:
            send_own(message(1, half, 0))
        energy(step, half)
        if send:
            send_own(message(1, half, 1))

    barrier = pltpu.get_barrier_semaphore()
    pl.semaphore_signal(barrier, inc=1, device_id=(other,), device_id_type=MESH)

    @pl.when(above)
    def _():
        pl.semaphore_signal(barrier, inc=1, device_id=(ahead,), device_id_type=MESH)

    @pl.when(below)
    def _():
        pl.semaphore_signal(barrier, inc=1, device_id=(behind,), device_id_type=MESH)

    @pl.when(near_across == 1)
    def _():
        pl.semaphore_signal(barrier, inc=1, device_id=(across,), device_id_type=MESH)

    tables = [
        pltpu.make_async_copy(source, target, table_sem.at[place])
        for place, (source, target) in enumerate(
            ((couplings_hbm, couplings), (k_hbm, k_table), (lam_hbm, lam_table), (top_hbm, top_ref))
        )
    ]
    tables[0].start()
    for half in range(HALVES):
        for field in range(3):
            for block in range(BLOCKS):
                load(half, field, block).start()
    for table in tables[1:]:
        table.start()
    pl.semaphore_wait(barrier, 1 + above.astype(jnp.int32) + below.astype(jnp.int32) + near_across)

    for table in tables:
        table.wait()
    first_sends(0)
    prepare(0, 0)
    clear()
    relay(0, 0)
    first_sends(1)
    prepare(0, 1)
    early(0, 0)
    late(0, 0)
    water(0, 0)
    energy(0, 0)
    relay(0, 1)
    send_own(message(1, 0, 0))
    send_own(message(1, 0, 1))
    prepare(1, 0)
    early(0, 1)
    late(0, 1)
    relay(1, 0, (0,))
    solve(0, 1, True)
    relay(1, 0, (1,))
    prepare(1, 1)
    early(1, 0)
    relay(1, 1)
    early(1, 1)
    late(1, 0)
    solve(1, 0)
    for field in range(2):
        for block in range(BLOCKS):
            store(0, field, block).start()
            for half in range(HALVES):
                store_base(half, field, block).start()
    late(1, 1)
    solve(1, 1)
    for field in range(2):
        for block in range(BLOCKS):
            store(1, field, block).start()
    for kind in range(COPIES):

        def action(kind=kind):
            ref = rx.at[W] if kind in (W, P1X, M1X) else passed
            whole(kind, ref, arrival_sem(kind, 0)).wait_send()

        guarded(sends[kind], action)
    for place, ref in enumerate((result, own.at[NATURAL, pl.ds(6, 4)])):
        pltpu.make_async_copy(ref, ref, store_sem.at[place]).wait()


def solution(mesh):
    devices = mesh.shape["cols"]

    def on_device(head, warmth, kinds, top, couplings, k_sat, heat_cond):
        plane = (BLOCKS, ROWS, LANES)
        hbm = pl.BlockSpec(memory_space=pltpu.HBM)
        f32 = jnp.float32
        out = pltpu.VMEM((2,) + head.shape, f32)
        base, change = pl.pallas_call(
            functools.partial(kernel, devices),
            out_shape=(out, out),
            in_specs=[hbm] * 7,
            out_specs=(pl.BlockSpec(memory_space=pltpu.VMEM),) * 2,
            scratch_shapes=[
                pltpu.VMEM((3, MESSAGES) + plane, f32),
                pltpu.VMEM((SLOTS, MESSAGES) + plane, f32),
                pltpu.VMEM((MESSAGES, ROWS, LANES), f32),
                pltpu.VMEM((HALVES, 2) + plane, f32),
                pltpu.VMEM((HALVES,) + plane, jnp.int32),
                pltpu.VMEM((HALVES,) + plane, f32),
                pltpu.VMEM((2, HALVES) + plane, f32),
                pltpu.VMEM((HALVES,) + plane, f32),
                pltpu.VMEM((HALVES,) + plane, f32),
                pltpu.VMEM((HALVES,) + plane, f32),
                pltpu.VMEM((HALVES,) + plane, f32),
                pltpu.VMEM((HALVES,) + plane, f32),
                pltpu.VMEM((CHUNK, BLOCKS, 8, LANES), f32),
                pltpu.VMEM((CHUNK, BLOCKS, 8, LANES), f32),
                pltpu.VMEM((CHUNK, BLOCKS, 8, LANES), f32),
                pltpu.VMEM((BLOCKS * HALVES, LANES), f32),
                pltpu.SMEM(couplings.shape, jnp.int32),
                pltpu.SMEM(k_sat.shape, f32),
                pltpu.SMEM(heat_cond.shape, f32),
                pltpu.SemaphoreType.DMA((4,)),
                pltpu.SemaphoreType.DMA((HALVES, 3)),
                pltpu.SemaphoreType.DMA((2,)),
                pltpu.SemaphoreType.DMA((COPIES,)),
                pltpu.SemaphoreType.DMA((len(SINGLE), MESSAGES)),
                pltpu.SemaphoreType.DMA((len(GROUPED), 4)),
            ],
            compiler_params=pltpu.CompilerParams(
                collective_id=0, has_side_effects=True, vmem_limit_bytes=65900000
            ),
        )(head, warmth, kinds, top.reshape(BLOCKS * HALVES, LANES), couplings, k_sat, heat_cond)
        return base[0] + change[0], base[1] + change[1]

    placed = (P(None, "cols"), P(None, "cols"), P(None, "cols"), P("cols"), P(), P(), P())
    return jax.shard_map(
        on_device,
        mesh=mesh,
        in_specs=placed,
        out_specs=(P(None, "cols"), P(None, "cols")),
        check_vma=False,
    )
```
